512 devices in a mesh: filter: 32 (over z_lo, x), space: 16 (over z_hi, y, core).
Axes of the slice: x: 4, y: 4, z: 16 (z_hi: 2, z_lo: 8; z = z_hi * 8 + z_lo), core: 2. Of those that a mesh axis runs over, the one named last changes fastest.
Arguments:
- volume: bfloat16 [1024, 64, 1024], P('filter', 'space'), may hold values from -6 to 6
- mixing: bfloat16 [1024, 1024], P('filter'), may hold values from -0.1875 to 0.1875
- kernel_taps: float32 [1024, 27], P('filter'), may hold values from -1.25 to 1.25
- upstream: bfloat16 [1024, 64, 1024], P('filter', 'space'), may hold values from -6 to 6
Outputs:
- output: bfloat16 [1024, 64, 1024], P('filter', 'space')
- volume_grad: bfloat16 [1024, 64, 1024], P('filter', 'space')
- mixing_grad: float32 [1024, 1024], P('filter', 'space')
- taps_grad: float32 [1024, 27], P('filter')
The draws below stay inside these ranges and needn't reach their ends.
All inputs are finite; a program needn't handle non-finite values.
Results may differ from the reference program's by a relative error of at most 0.0055.
Values may be sent and summed in bfloat16 or wider, within the bound.
A program may use at most 64 MiB of HBM per device.

```python
import math
import jax
import jax.numpy as jnp
from jax import lax

C = 1024
HH = 16
WW = 64
D = 64
HW = 1024


def with_spikes(values, key, source, target, parts, factor):
    def block_of(position):
        return (jnp.arange(values.shape[position]) // (values.shape[position] // parts)).reshape((-1,) + (1,) * (values.ndim - 1 - position))

    near = jax.random.permutation(key, parts)[block_of(target)]
    other_side = (block_of(target) + parts // 2) % parts
    return jnp.where((block_of(source) == near) | (block_of(source) == other_side), factor * values, values)


def block_scale(rng, shape, shards, low, top_value):
    def one(dim, shards_of):
        steps = jax.random.uniform(jax.random.fold_in(jax.random.fold_in(rng, 6), dim), (shards_of,), jnp.float32, low / len(shards), top_value / len(shards))
        return jnp.repeat(jnp.exp(steps), shape[dim] // shards_of).reshape((-1,) + (1,) * (len(shape) - dim - 1))

    loudness = one(*shards[0])
    for cut in shards[1:]:
        loudness = loudness * one(*cut)
    return loudness


def scatter_about(rng, dims, spread, bound, shards=(), kind=jnp.bfloat16):
    drawn = spread * jax.random.normal(rng, dims, jnp.float32)
    if shards:
        drawn = drawn * block_scale(rng, dims, shards, -0.22, 0.18)
    return jnp.clip(drawn, -bound, bound).astype(kind)


def heavy_noise(key, shape, deviation, bound, shards, heavy, held_as=jnp.bfloat16):
    values = deviation * jax.random.normal(key, shape, jnp.float32)
    if shards:
        values = values * block_scale(key, shape, shards, -0.22, 0.18)
    return jnp.clip(with_spikes(values, jax.random.fold_in(key, 3), *heavy), -bound, bound).astype(held_as)


def setup_inputs(seed: int = 0) -> dict:
    key_list = jax.random.split(jax.random.key(seed), 5)
    return {
        "volume": heavy_noise(key_list[0], (C, D, HW), 1.0, 6.0, ((0, 32), (1, 16)), (1, 0, 32, 2.75)),
        "mixing": scatter_about(key_list[1], (C, C), C ** -0.5, 0.1875, ((0, 32),)),
        "kernel_taps": scatter_about(key_list[2], (C, 27), 27 ** -0.5, 1.25, ((0, 32),), jnp.float32),
        "upstream": scatter_about(key_list[3], (C, D, HW), 1.0, 6.0, ((0, 32), (1, 16))),
    }


def pad_sides(field):
    return jnp.pad(field, ((0, 0), (1, 1), (1, 1), (1, 1)))

def depth_conv(padded, kernel_taps, flip):
    depth = padded.shape[1] - 2
    height = padded.shape[2] - 2
    breadth = padded.shape[3] - 2
    summed = jnp.zeros((padded.shape[0], depth, height, breadth), jnp.float32)
    for plane_off in range(3):
        for row_off in range(3):
            for col_off in range(3):
                index_tap = plane_off * 9 + row_off * 3 + col_off
                if flip:
                    plane_at, row_at, col_at = (2 - plane_off, 2 - row_off, 2 - col_off)
                else:
                    plane_at, row_at, col_at = (plane_off, row_off, col_off)
                window = padded[:, plane_at:plane_at + depth, row_at:row_at + height, col_at:col_at + breadth]
                summed = summed + kernel_taps[:, index_tap][:, None, None, None] * window.astype(jnp.float32)
    return summed

def tap_grads(grad_field, padded):
    depth = grad_field.shape[1]
    height = grad_field.shape[2]
    breadth = grad_field.shape[3]
    grad_wide = grad_field.astype(jnp.float32)
    columns_list = []
    for plane_off in range(3):
        for row_off in range(3):
            for col_off in range(3):
                window = padded[:, plane_off:plane_off + depth, row_off:row_off + height, col_off:col_off + breadth]
                columns_list.append(lax.optimization_barrier(jnp.sum(grad_wide * window.astype(jnp.float32), axis=(1, 2, 3))))
    return jnp.stack(columns_list, axis=1)

def silu_slope(values):
    sig_val = jax.nn.sigmoid(values)
    return sig_val * (1.0 + values * (1.0 - sig_val))

def reference(volume, mixing, kernel_taps, upstream):
    channels = volume.shape[0]
    flat_vol = volume.reshape(channels, D * HW)
    mixed = jnp.dot(mixing, flat_vol, preferred_element_type=jnp.float32).astype(jnp.bfloat16)
    mixed_pad = pad_sides(mixed.reshape(channels, D, HH, WW))
    spatial = depth_conv(mixed_pad, kernel_taps, False)
    vol_grid = volume.reshape(channels, D, HH, WW).astype(jnp.float32)
    output = (vol_grid + jax.nn.silu(spatial)).astype(jnp.bfloat16).reshape(channels, D, HW)
    up_grid = upstream.reshape(channels, D, HH, WW).astype(jnp.float32)
    spatial_grad = (up_grid * silu_slope(spatial)).astype(jnp.bfloat16)
    mixed_grad = depth_conv(pad_sides(spatial_grad), kernel_taps, True).astype(jnp.bfloat16).reshape(channels, D * HW)
    norm_factor = 1.0 / math.sqrt(D * HH * WW)
    back_sum = jnp.dot(mixing.T, mixed_grad, preferred_element_type=jnp.float32)
    volume_grad = (upstream.reshape(channels, D * HW).astype(jnp.float32) + back_sum).astype(jnp.bfloat16).reshape(channels, D, HW)
    mixing_grad = jnp.dot(mixed_grad, flat_vol.T, preferred_element_type=jnp.float32) * norm_factor
    taps_grad = tap_grads(spatial_grad, mixed_pad) * norm_factor
    return (output, volume_grad, mixing_grad, taps_grad)
```

```python
import functools
import math

import jax
import jax.numpy as jnp
from jax import lax
from jax.experimental import pallas as pl
from jax.experimental.pallas import tpu as pltpu
from jax.sharding import PartitionSpec as P

F32 = jnp.float32
BF16 = jnp.bfloat16
MESH = pl.DeviceIdType.MESH

NZ, NX, NY = 8, 4, 4
NF, NS = 32, 16
CH = 32
PLANES, CELLS, WW = 4, 1024, 64
SLAB = PLANES * CELLS
PART = SLAB // NZ
C = NF * CH
HALF = PART // 2
ORDER = (4, 3, 5, 2, 6, 1, 7)


class Slots:
    def __init__(self):
        self.used = 0

    def take(self, n):
        first = self.used
        self.used += n
        return first


N_SEMS = 330


def kernel(
    norm, vol, up, mix, taps, out, vgrad, mgrad, tgrad,
    vol_all, mg_all, wall, wt, mq, bq, mb, m32, sg32, sp32, sgb, sgh, mgb, bb, tb, tg, ts, tr,
    dw, d1, a1b, d2, a2, a2b, d3, d4s, d4r, sems,
):
    f = lax.axis_index("filter")
    s = lax.axis_index("space")

    def div(a, b):
        return lax.div(a, jnp.int32(b))

    def rem(a, b):
        return lax.rem(a, jnp.int32(b))

    zl, x = div(f, NX), rem(f, NX)
    zh, c = div(s, 8), rem(s, 2)
    y = div(rem(s, 8), 2)
    xr, xl, xo = rem(x + 1, NX), rem(x + 3, NX), rem(x + 2, NX)
    s_c = s + 1 - 2 * c
    s_n = rem(s + 15 + 2 * c, NS)
    s_h = rem(s + 8, NS)

    def at(zl_, x_, s_):
        return {"filter": zl_ * NX + x_, "space": s_}

    def lanes(start, size):
        return pl.ds(pl.multiple_of(start, 128), size)

    slots = Slots()
    pending = []

    def copy_to(src, dst, ss, rs, where):
        return pltpu.make_async_remote_copy(
            src_ref=src, dst_ref=dst, send_sem=sems.at[ss], recv_sem=sems.at[rs],
            device_id=where, device_id_type=MESH,
        )

    def send(src, dst, ss, rs, where):
        cp = copy_to(src, dst, ss, rs, where)
        cp.start()
        pending.append(cp)

    def recv(dst, rs, where):
        copy_to(dst, dst, rs, rs, where).wait_recv()

    barrier = pltpu.get_barrier_semaphore()
    peers = [at(rem(zl + t, NZ), x, s) for t in range(1, NZ)]
    peers += [at(rem(zl + t, NZ), x, s_h) for t in range(NZ)]
    peers += [at(zl, rem(x + t, NX), s) for t in range(1, NX)]
    peers += [at(zl, x, s_c), at(zl, x, s_n)]
    peers += [at(zl, x, zh * 8 + rem(y + t, NY) * 2 + c) for t in range(1, NY)]
    for peer in peers:
        pl.semaphore_signal(barrier, inc=1, device_id=peer, device_id_type=MESH)
    pl.semaphore_wait(barrier, len(peers))

    class Gather:
        def __init__(self, src, dst):
            self.src, self.dst = src, dst
            self.zs, self.zr = slots.take(NZ), slots.take(NZ)
            self.fs = [slots.take(NZ), slots.take(NZ)]
            self.fr = [slots.take(NZ), slots.take(NZ)]
            self.rs = [slots.take(NZ), slots.take(NZ)]
            self.rr = [slots.take(NZ), slots.take(NZ)]

        def forward(self, src, zf, t):
            send(src, self.dst.at[zf, x], self.fs[0] + t, self.fr[0] + t, at(zl, xr, s))
            send(src, self.dst.at[zf, x], self.fs[1] + t, self.fr[1] + t, at(zl, xl, s))

        def start(self):
            for t in ORDER:
                zt = rem(zl + t, NZ)
                send(self.src.at[:, lanes(PART * zt, PART)], self.dst.at[zl, x],
                     self.zs + t, self.zr + t, at(zt, x, s))
            self.forward(self.src.at[:, lanes(PART * zl, PART)], zl, 0)
            self.dst[zl, x] = self.src[:, lanes(PART * zl, PART)]

        def arrive(self, t):
            zf = rem(zl + NZ - t, NZ)
            recv(self.dst.at[zf, x], self.zr + t, at(zf, x, s))
            self.forward(self.dst.at[zf, x], zf, t)

        def relay(self, t):
            zf = rem(zl + NZ - t, NZ)
            low, high = pl.ds(0, HALF), pl.ds(HALF, HALF)
            recv(self.dst.at[zf, xl], self.fr[0] + t, at(zl, xl, s))
            part = self.dst.at[zf, xl, :, low]
            send(part, part, self.rs[0] + t, self.rr[0] + t, at(zl, xr, s))
            recv(self.dst.at[zf, xr], self.fr[1] + t, at(zl, xr, s))
            part = self.dst.at[zf, xr, :, high]
            send(part, part, self.rs[1] + t, self.rr[1] + t, at(zl, xl, s))

        def finish(self):
            for t in (0,) + ORDER:
                zf = rem(zl + NZ - t, NZ)
                recv(self.dst.at[zf, xo, :, pl.ds(0, HALF)], self.rr[0] + t, at(zl, xl, s))
                recv(self.dst.at[zf, xo, :, pl.ds(HALF, HALF)], self.rr[1] + t, at(zl, xr, s))

    class Scatter:
        def __init__(self, src, dst, offset):
            self.src, self.dst, self.offset = src, dst, offset
            self.ss, self.sr = slots.take(NZ), slots.take(NZ)

        def place(self, z):
            return self.dst.at[:, lanes(self.offset + PART * z, PART)]

        def start(self):
            for t in ORDER:
                zt = rem(zl + t, NZ)
                send(self.src.at[zt], self.place(zl), self.ss + t, self.sr + zl, at(zt, x, s))
            self.dst[:, lanes(self.offset + PART * zl, PART)] = self.src[zl]

        def wait(self, z):
            @pl.when(zl != z)
            def _():
                recv(self.place(z), self.sr + z, at(z, x, s))

    k = c * 4 + y
    own_cols = lanes(128 * k, 128)
    side = lanes(512 * c, 512)
    other = lanes(512 * (1 - c), 512)
    w1s, w1r = slots.take(NZ), slots.take(NZ)
    w2s, w2r = slots.take(NY), slots.take(NY)
    w3s, w3r = slots.take(1), slots.take(1)
    w4s, w4r = slots.take(NX), slots.take(NX)
    w5s, w5r = slots.take(NX), slots.take(NX)

    def space_y(t):
        return zh * 8 + rem(y + t, NY) * 2 + c

    def w1_start():
        for t in ORDER:
            send(mix.at[:, own_cols], wall.at[zl, x, :, own_cols], w1s + t, w1r + t, at(rem(zl + t, NZ), x, s))
        wall[zl, x, :, own_cols] = mix[:, own_cols]

    def w2_start():
        for t in ORDER:
            zf = rem(zl + NZ - t, NZ)
            recv(wall.at[zf, x, :, own_cols], w1r + t, at(zf, x, s))
        part = wall.at[:, x, :, own_cols]
        for t in range(1, NY):
            send(part, part, w2s + t, w2r + t, at(zl, x, space_y(t)))

    def w3_start():
        for t in range(1, NY):
            cols = lanes(128 * (c * 4 + rem(y + NY - t, NY)), 128)
            recv(wall.at[:, x, :, cols], w2r + t, at(zl, x, space_y(NY - t)))
        part = wall.at[:, x, :, side]
        send(part, part, w3s, w3r, at(zl, x, s_c))

    def w3_wait():
        recv(wall.at[:, x, :, other], w3r, at(zl, x, s_c))

    def w4_start():
        part = wall.at[:, x, :, side]
        for t in range(1, NX):
            send(part, part, w4s + t, w4r + t, at(zl, rem(x + t, NX), s))

    def w5_start():
        for t in range(1, NX):
            xf = rem(x + NX - t, NX)
            part = wall.at[:, xf, :, side]
            recv(part, w4r + t, at(zl, xf, s))
            send(part, part, w5s + t, w5r + t, at(zl, x, s_c))

    def w5_wait():
        for t in range(1, NX):
            xf = rem(x + NX - t, NX)
            recv(wall.at[:, xf, :, other], w5r + t, at(zl, x, s_c))

    lane = lax.broadcasted_iota(jnp.int32, (8, 8, 128), 2)
    first_col = lax.rem(lane, WW) == 0
    last_col = lax.rem(lane, WW) == WW - 1
    first_row = lane < WW
    zero = jnp.zeros((8, 8, 128), F32)

    def columns(v):
        before = jnp.where(first_col, zero, pltpu.roll(v, 1, 2))
        after = jnp.where(last_col, zero, pltpu.roll(v, 127, 2))
        return before, v, after

    def rows_down(v):
        swapped = pltpu.roll(v, WW, 2)
        above = jnp.concatenate([zero[:1], swapped[:-1]], axis=0)
        return jnp.where(first_row, above, swapped)

    def rows_up(v):
        swapped = pltpu.roll(v, WW, 2)
        below = jnp.concatenate([swapped[1:], zero[:1]], axis=0)
        return jnp.where(first_row, swapped, below)

    def conv(src, d, flip):
        @pl.loop(0, CH // 8)
        def _(g):
            rows = pl.ds(pl.multiple_of(8 * g, 8), 8)
            sums = [None] * 3
            for a in range(3):
                shifted = columns(src[pl.ds(8 * (d + a), 8), rows, :])
                for b in range(3):
                    for e in range(3):
                        tap = 9 * a + 3 * b + e
                        tap = 26 - tap if flip else tap
                        term = tb[tap, rows, :][None] * shifted[e]
                        sums[b] = term if sums[b] is None else sums[b] + term
            sp32[pl.ds(8 * d, 8), rows, :] = rows_down(sums[0]) + sums[1] + rows_up(sums[2])

    def widen(src, start, dst, chunk):
        for j in range(8):
            dst[chunk + j] = src[:, pl.ds(start + 128 * j, 128)].astype(F32)

    def pointwise(d):
        @pl.loop(0, 8)
        def _(j):
            at_chunk = 8 * d + j
            cells = lanes(128 * at_chunk, 128)
            spatial = sp32[at_chunk]
            sig = lax.logistic(spatial)
            grad = up[:, cells].astype(F32) * (sig * (1.0 + spatial * (1.0 - sig)))
            grad = grad.astype(BF16)
            sgb[:, cells] = grad
            sg32[8 + at_chunk] = grad.astype(F32)
            out[:, cells] = (vol[:, cells].astype(F32) + spatial * sig).astype(BF16)

    def forward_planes(first, step):
        @pl.loop(0, 2)
        def _(i):
            d = first + step * i
            conv(m32, d, False)
            pointwise(d)

    def backward_planes(first, step):
        @pl.loop(0, 2)
        def _(i):
            d = first + step * i
            conv(sg32, d, True)

            @pl.loop(0, 8)
            def _(j):
                mgb[:, lanes(128 * (8 * d + j), 128)] = sp32[8 * d + j].astype(BF16)

    def tap_sums():
        @pl.loop(0, CH // 8)
        def _(g):
            rows = pl.ds(pl.multiple_of(8 * g, 8), 8)
            for tap in range(27):
                tg[tap, rows, :] = zero[0]

            @pl.loop(0, PLANES)
            def _(d):
                grad = sg32[pl.ds(8 * d + 8, 8), rows, :]
                grads = (rows_up(grad), grad, rows_down(grad))
                for a in range(3):
                    shifted = columns(m32[pl.ds(8 * (d + a), 8), rows, :])
                    for b in range(3):
                        for e in range(3):
                            tap = 9 * a + 3 * b + e
                            tg[tap, rows, :] = tg[tap, rows, :] + jnp.sum(grads[b] * shifted[e], axis=0)

        tap_lane = lax.broadcasted_iota(jnp.int32, (CH, 128), 1)
        total = jnp.zeros((CH, 128), F32)
        for tap in range(27):
            total = jnp.where(tap_lane == tap, jnp.sum(tg[tap], axis=1, keepdims=True), total)
        ts[0] = total

    halo_s = [slots.take(2), slots.take(2)]
    halo_r = [slots.take(2), slots.take(2)]
    has_low, has_high = s > 0, s < NS - 1

    def halo_low(i, src, dst):
        return copy_to(src, dst, halo_s[i], halo_r[i], at(zl, x, s - 1))

    def halo_high(i, src, dst):
        return copy_to(src, dst, halo_s[i] + 1, halo_r[i] + 1, at(zl, x, s + 1))

    def m_low():
        return halo_low(0, mb.at[:, pl.ds(CELLS, CELLS)], mb.at[:, pl.ds(5 * CELLS, CELLS)])

    def m_high():
        return halo_high(0, mb.at[:, pl.ds(4 * CELLS, CELLS)], mb.at[:, pl.ds(0, CELLS)])

    def g_low():
        return halo_low(1, sgb.at[:, pl.ds(0, CELLS)], sgh.at[:, pl.ds(CELLS, CELLS)])

    def g_high():
        return halo_high(1, sgb.at[:, pl.ds(3 * CELLS, CELLS)], sgh.at[:, pl.ds(0, CELLS)])

    def halo_arrive(i, low_ref, low_at, high_ref, high_at, dst):
        @pl.when(has_low)
        def _():
            recv(low_ref.at[:, pl.ds(low_at, CELLS)], halo_r[i] + 1, at(zl, x, s - 1))
            widen(low_ref, low_at, dst, 0)

        @pl.when(s == 0)
        def _():
            for j in range(8):
                dst[j] = jnp.zeros((CH, 128), F32)

        @pl.when(has_high)
        def _():
            recv(high_ref.at[:, pl.ds(high_at, CELLS)], halo_r[i], at(zl, x, s + 1))
            widen(high_ref, high_at, dst, 40)

        @pl.when(s == NS - 1)
        def _():
            for j in range(8):
                dst[40 + j] = jnp.zeros((CH, 128), F32)

    volume_gather = Gather(vol, vol_all)
    grad_gather = Gather(mgb, mg_all)
    mixed_scatter = Scatter(mq, mb, CELLS)
    back_scatter = Scatter(bq, bb, 0)

    w1_start()
    volume_gather.start()
    for tap in range(27):
        tb[tap] = jnp.broadcast_to(taps[:, tap : tap + 1], (CH, 128))
    hooks = {1: w2_start, 4: w3_start}
    volume_gather.relay(0)
    for i, t in enumerate(ORDER):
        volume_gather.arrive(t)
        if i in hooks:
            hooks[i]()
        if i:
            volume_gather.relay(ORDER[i - 1])
    volume_gather.relay(ORDER[-1])
    w3_wait()
    volume_gather.finish()
    columns_own = wall[:, pl.ds(x, 1), :, :].reshape(NZ * CH, C)
    mixed = jnp.dot(columns_own, vol_all[...].reshape(C, PART), preferred_element_type=F32)
    mq[...] = mixed.astype(BF16).reshape(NZ, CH, PART)
    mixed_scatter.start()
    w4_start()
    for z in (0, 1):
        mixed_scatter.wait(z)
    pl.when(has_low)(lambda: m_low().start())
    for z in (6, 7):
        mixed_scatter.wait(z)
    pl.when(has_high)(lambda: m_high().start())
    for z in (2, 3, 4, 5):
        mixed_scatter.wait(z)

    for d in range(PLANES):
        widen(mb, CELLS * (d + 1), m32, 8 * (d + 1))
    forward_planes(1, 1)
    halo_arrive(0, mb, 0, mb, 5 * CELLS, m32)
    forward_planes(0, 3)
    pl.when(has_low)(lambda: g_low().start())
    pl.when(has_high)(lambda: g_high().start())
    w5_start()

    backward_planes(1, 1)
    tap_sums()
    halo_arrive(1, sgh, 0, sgh, CELLS, sg32)
    backward_planes(0, 3)
    grad_gather.start()

    t1s, t1r = slots.take(1), slots.take(1)
    t2s, t2r = slots.take(NY), slots.take(NY)
    t3s, t3r = slots.take(1), slots.take(1)
    send(ts.at[0], tr.at[0], t1s, t1r, at(zl, x, s_c))

    def taps_y():
        recv(tr.at[0], t1r, at(zl, x, s_c))
        ts[1] = ts[0] + tr[0]
        for t in range(1, NY):
            send(ts.at[1], tr.at[1 + y], t2s + t, t2r + t, at(zl, x, space_y(t)))
        tr[1 + y] = ts[1]

    def taps_z():
        for t in range(1, NY):
            recv(tr.at[1 + rem(y + NY - t, NY)], t2r + t, at(zl, x, space_y(NY - t)))
        ts[2] = (tr[1] + tr[2]) + (tr[3] + tr[4])
        send(ts.at[2], tr.at[5], t3s, t3r, at(zl, x, s_h))

    w5_wait()
    for z in range(NZ):
        block = wall[:, :, :, pl.ds(128 * z, 128)].reshape(C, 128)
        wt[z] = block.T.reshape(NX, CH, C)

    hooks = {2: taps_y, 5: taps_z}
    grad_gather.relay(0)
    for i, t in enumerate(ORDER):
        grad_gather.arrive(t)
        if i in hooks:
            hooks[i]()
        if i:
            grad_gather.relay(ORDER[i - 1])
    grad_gather.relay(ORDER[-1])

    d1s, d1r = slots.take(1), slots.take(1)
    d2s, d2r = slots.take(2 * NY), slots.take(2 * NY)
    d3s, d3r = slots.take(NS), slots.take(NS)
    d4s_sem, d4r_sem = slots.take(1), slots.take(1)
    own_grad = mg_all[:, pl.ds(x, 1), :, :].reshape(NZ * CH, PART)
    for i in range(4):
        part = lax.dot_general(
            own_grad, vol_all[pl.ds(2 * i, 2)].reshape(C // 4, PART),
            (((1,), (1,)), ((), ())), preferred_element_type=F32,
        )
        dw[:, :, :, pl.ds(256 * i, 256)] = part.reshape(NZ, 2, CH // 2, C // 4)
    send(dw.at[:, 1 - c], d1, d1s, d1r, at(zl, x, s_c))

    grad_gather.finish()
    rows_own = wt[:, pl.ds(x, 1), :, :].reshape(NZ * CH, C)
    back = jnp.dot(rows_own, mg_all[...].reshape(C, PART), preferred_element_type=F32)
    bq[...] = back.astype(BF16).reshape(NZ, CH, PART)
    back_scatter.start()

    recv(d1, d1r, at(zl, x, s_c))
    summed = d1[...] + dw[:, pl.ds(c, 1)].reshape(NZ, CH // 2, C)
    d1[...] = summed
    a1b[...] = summed.astype(BF16)
    for t in range(1, NY):
        for h in range(2):
            cols = lanes(128 * (4 * h + rem(y + t, NY)), 128)
            send(a1b.at[:, :, cols], d2.at[t - 1, h], d2s + 2 * t + h, d2r + 2 * t + h, at(zl, x, space_y(t)))
    for h in range(2):
        summed = d1[:, :, lanes(128 * (4 * h + y), 128)]
        for t in range(1, NY):
            recv(d2.at[t - 1, h], d2r + 2 * t + h, at(zl, x, space_y(NY - t)))
            summed = summed + d2[t - 1, h].astype(F32)
        a2[h] = summed
        a2b[h] = summed.astype(BF16)
    z_own = zh * NZ + zl

    def ring(t):
        z = rem(z_own + t, NS)
        return div(z, NZ), rem(z, NZ)

    for t in (8, 7, 9, 6, 10, 5, 11, 4, 12, 3, 13, 2, 14, 1, 15):
        h, z = ring(t)
        send(a2b.at[h, z], d3.at[t - 1], d3s + t, d3r + t, at(z, x, h * 8 + y * 2 + c))
    total = a2[zh, zl]
    for t in range(1, NS):
        h, z = ring(NS - t)
        recv(d3.at[t - 1], d3r + t, at(z, x, h * 8 + y * 2 + c))
        total = total + d3[t - 1].astype(F32)
    d4s[...] = total
    send(d4s, d4r, d4s_sem, d4r_sem, at(zl, x, s_c))

    for z in range(NZ):
        back_scatter.wait(z)

    @pl.loop(0, SLAB // 128)
    def _(j):
        cells = lanes(128 * j, 128)
        vgrad[:, cells] = (up[:, cells].astype(F32) + bb[:, cells].astype(F32)).astype(BF16)

    recv(tr.at[5], t3r, at(zl, x, s_h))
    tgrad[...] = ((ts[2] + tr[5]) * norm)[:, :27]
    recv(d4r, d4r_sem, at(zl, x, s_c))
    even = c == 0
    full = jnp.concatenate(
        [jnp.where(even, d4s[...], d4r[...]), jnp.where(even, d4r[...], d4s[...])], axis=0
    )
    mgrad[...] = jnp.where(even, full[:, :64], full[:, 64:]) * norm

    for cp in pending:
        cp.wait_send()
    for low, high in ((m_low, m_high), (g_low, g_high)):
        pl.when(has_low)(lambda low=low: low().wait_send())
        pl.when(has_high)(lambda high=high: high().wait_send())
    assert slots.used <= N_SEMS


def body(volume, mixing, kernel_taps, upstream):
    norm = 1.0 / math.sqrt(PLANES * NS * CELLS)
    vmem = pl.BlockSpec(memory_space=pltpu.VMEM)
    scratch = [
        ((NZ, NX, CH, PART), BF16),
        ((NZ, NX, CH, PART), BF16),
        ((NZ, NX, CH, C), BF16),
        ((NZ, NX, CH, C), BF16),
        ((NZ, CH, PART), BF16),
        ((NZ, CH, PART), BF16),
        ((CH, 6 * CELLS), BF16),
        ((48, CH, 128), F32),
        ((48, CH, 128), F32),
        ((32, CH, 128), F32),
        ((CH, SLAB), BF16),
        ((CH, 2 * CELLS), BF16),
        ((CH, SLAB), BF16),
        ((CH, SLAB), BF16),
        ((27, CH, 128), F32),
        ((27, CH, 128), F32),
        ((3, CH, 128), F32),
        ((6, CH, 128), F32),
        ((NZ, 2, CH // 2, C), F32),
        ((NZ, CH // 2, C), F32),
        ((NZ, CH // 2, C), BF16),
        ((3, 2, NZ, CH // 2, 128), BF16),
        ((2, NZ, CH // 2, 128), F32),
        ((2, NZ, CH // 2, 128), BF16),
        ((NS - 1, CH // 2, 128), BF16),
        ((CH // 2, 128), F32),
        ((CH // 2, 128), F32),
    ]
    output, volume_grad, mixing_grad, taps_grad = pl.pallas_call(
        functools.partial(kernel, norm),
        out_shape=(
            jax.ShapeDtypeStruct((CH, SLAB), BF16),
            jax.ShapeDtypeStruct((CH, SLAB), BF16),
            jax.ShapeDtypeStruct((CH, C // NS), F32),
            jax.ShapeDtypeStruct((CH, 27), F32),
        ),
        in_specs=[vmem] * 4,
        out_specs=(vmem,) * 4,
        scratch_shapes=[pltpu.VMEM(*one) for one in scratch] + [pltpu.SemaphoreType.DMA((N_SEMS,))],
        compiler_params=pltpu.CompilerParams(collective_id=0, has_side_effects=True),
        name="conv_block",
    )(volume.reshape(CH, SLAB), upstream.reshape(CH, SLAB), mixing, kernel_taps)
    shape = (CH, PLANES, CELLS)
    return output.reshape(shape), volume_grad.reshape(shape), mixing_grad, taps_grad


def solution(mesh):
    channel_slab = P("filter", "space", None)
    return jax.shard_map(
        body,
        mesh=mesh,
        in_specs=(channel_slab, P("filter", None), P("filter", None), channel_slab),
        out_specs=(channel_slab, channel_slab, P("filter", "space"), P("filter", None)),
        check_vma=False,
    )
```

```python
import functools
import math

import jax
import jax.numpy as jnp
from jax import lax
from jax.experimental import pallas as pl
from jax.experimental.pallas import tpu as pltpu
from jax.sharding import PartitionSpec as P

F32 = jnp.float32
BF16 = jnp.bfloat16
MESH = pl.DeviceIdType.MESH

NZ, NX, NY = 8, 4, 4
NF, NS = 32, 16
CH = 32
PLANES, CELLS, WW = 4, 1024, 64
SLAB = PLANES * CELLS
PART = SLAB // NZ
C = NF * CH
CHUNKS = 4
WIDTH = PART // CHUNKS
ORDER = (4, 3, 5, 2, 6, 1, 7)


class Slots:
    def __init__(self):
        self.used = 0

    def take(self, n):
        first = self.used
        self.used += n
        return first


N_SEMS = 440


def kernel(
    norm, vol, up, mix, taps, out, vgrad, mgrad, tgrad,
    vol_all, mg_all, wall, wt, mq, bq, mb, m32, sg32, sp32, sgb, sgh, mgb, bb, tb, tg, ts, tr,
    dw, d1, a1b, d2, a2, a2b, d3, d4s, d4r, sems,
):
    f = lax.axis_index("filter")
    s = lax.axis_index("space")

    def div(a, b):
        return lax.div(a, jnp.int32(b))

    def rem(a, b):
        return lax.rem(a, jnp.int32(b))

    zl, x = div(f, NX), rem(f, NX)
    zh, c = div(s, 8), rem(s, 2)
    y = div(rem(s, 8), 2)
    s_c = s + 1 - 2 * c
    s_n = rem(s + 15 + 2 * c, NS)
    s_h = rem(s + 8, NS)

    def at(zl_, x_, s_):
        return {"filter": zl_ * NX + x_, "space": s_}

    def lanes(start, size):
        return pl.ds(pl.multiple_of(start, 128), size)

    def chunk(j):
        return pl.ds(WIDTH * j, WIDTH)

    slots = Slots()
    pending = []

    def copy_to(src, dst, ss, rs, where):
        return pltpu.make_async_remote_copy(
            src_ref=src, dst_ref=dst, send_sem=sems.at[ss], recv_sem=sems.at[rs],
            device_id=where, device_id_type=MESH,
        )

    def send(src, dst, ss, rs, where):
        cp = copy_to(src, dst, ss, rs, where)
        cp.start()
        pending.append(cp)

    def recv(dst, rs, where):
        copy_to(dst, dst, rs, rs, where).wait_recv()

    barrier = pltpu.get_barrier_semaphore()
    peers = [at(rem(zl + t, NZ), x, s) for t in range(1, NZ)]
    peers += [at(rem(zl + t, NZ), x, s_h) for t in range(NZ)]
    peers += [at(zl, rem(x + t, NX), s) for t in range(1, NX)]
    peers += [at(zl, x, s_c), at(zl, x, s_n)]
    peers += [at(zl, x, zh * 8 + rem(y + t, NY) * 2 + c) for t in range(1, NY)]
    for peer in peers:
        pl.semaphore_signal(barrier, inc=1, device_id=peer, device_id_type=MESH)
    pl.semaphore_wait(barrier, len(peers))

    class Gather:
        def __init__(self, src, dst):
            self.src, self.dst = src, dst
            self.zs, self.zr = slots.take(NZ * CHUNKS), slots.take(NZ * CHUNKS)
            self.xs, self.xr = slots.take(NX * CHUNKS), slots.take(NX * CHUNKS)

        def start(self):
            for j in range(CHUNKS):
                for t in ORDER:
                    zt = rem(zl + t, NZ)
                    send(self.src.at[:, lanes(PART * zt + WIDTH * j, WIDTH)], self.dst.at[zl, x, :, chunk(j)],
                         self.zs + NZ * j + t, self.zr + NZ * j + t, at(zt, x, s))
            self.dst[zl, x] = self.src[:, lanes(PART * zl, PART)]

        def arrive(self, j):
            for t in ORDER:
                zf = rem(zl + NZ - t, NZ)
                recv(self.dst.at[zf, x, :, chunk(j)], self.zr + NZ * j + t, at(zf, x, s))
            part = self.dst.at[:, x, :, chunk(j)]
            for t in (2, 1, 3):
                send(part, part, self.xs + NX * j + t, self.xr + NX * j + t, at(zl, rem(x + t, NX), s))

        def finish(self, j):
            for t in (1, 3, 2):
                xf = rem(x + NX - t, NX)
                recv(self.dst.at[:, xf, :, chunk(j)], self.xr + NX * j + t, at(zl, xf, s))

    class Scatter:
        def __init__(self, src, dst, offset):
            self.src, self.dst, self.offset = src, dst, offset
            self.ss, self.sr = slots.take(NZ * CHUNKS), slots.take(NZ * CHUNKS)

        def place(self, z, j):
            return self.dst.at[:, lanes(self.offset + PART * z + WIDTH * j, WIDTH)]

        def start(self, j):
            for t in ORDER:
                zt = rem(zl + t, NZ)
                send(self.src.at[zt, :, chunk(j)], self.place(zl, j),
                     self.ss + NZ * j + t, self.sr + NZ * j + zl, at(zt, x, s))
            self.dst[:, lanes(self.offset + PART * zl + WIDTH * j, WIDTH)] = self.src[zl, :, chunk(j)]

        def wait(self, z):
            @pl.when(zl != z)
            def _():
                for j in range(CHUNKS):
                    recv(self.place(z, j), self.sr + NZ * j + z, at(z, x, s))

    def multiply(weights, data, j, dst):
        product = jnp.dot(weights, data[:, :, :, chunk(j)].reshape(C, WIDTH), preferred_element_type=F32)
        dst[:, :, chunk(j)] = product.astype(BF16).reshape(NZ, CH, WIDTH)

    k = c * 4 + y
    own_cols = lanes(128 * k, 128)
    side = lanes(512 * c, 512)
    other = lanes(512 * (1 - c), 512)
    w1s, w1r = slots.take(NZ), slots.take(NZ)
    w2s, w2r = slots.take(NY), slots.take(NY)
    w3s, w3r = slots.take(1), slots.take(1)
    w4s, w4r = slots.take(NX), slots.take(NX)
    w5s, w5r = slots.take(NX), slots.take(NX)

    def space_y(t):
        return zh * 8 + rem(y + t, NY) * 2 + c

    def w1_start():
        for t in ORDER:
            send(mix.at[:, own_cols], wall.at[zl, x, :, own_cols], w1s + t, w1r + t, at(rem(zl + t, NZ), x, s))
        wall[zl, x, :, own_cols] = mix[:, own_cols]

    def w2_start():
        for t in ORDER:
            zf = rem(zl + NZ - t, NZ)
            recv(wall.at[zf, x, :, own_cols], w1r + t, at(zf, x, s))
        part = wall.at[:, x, :, own_cols]
        for t in range(1, NY):
            send(part, part, w2s + t, w2r + t, at(zl, x, space_y(t)))

    def w3_start():
        for t in range(1, NY):
            cols = lanes(128 * (c * 4 + rem(y + NY - t, NY)), 128)
            recv(wall.at[:, x, :, cols], w2r + t, at(zl, x, space_y(NY - t)))
        part = wall.at[:, x, :, side]
        send(part, part, w3s, w3r, at(zl, x, s_c))

    def w3_wait():
        recv(wall.at[:, x, :, other], w3r, at(zl, x, s_c))

    def w4_start():
        part = wall.at[:, x, :, side]
        for t in range(1, NX):
            send(part, part, w4s + t, w4r + t, at(zl, rem(x + t, NX), s))

    def w5_start():
        for t in range(1, NX):
            xf = rem(x + NX - t, NX)
            part = wall.at[:, xf, :, side]
            recv(part, w4r + t, at(zl, xf, s))
            send(part, part, w5s + t, w5r + t, at(zl, x, s_c))

    def w5_wait():
        for t in range(1, NX):
            xf = rem(x + NX - t, NX)
            recv(wall.at[:, xf, :, other], w5r + t, at(zl, x, s_c))

    lane = lax.broadcasted_iota(jnp.int32, (8, 8, 128), 2)
    first_col = lax.rem(lane, WW) == 0
    last_col = lax.rem(lane, WW) == WW - 1
    first_row = lane < WW
    zero = jnp.zeros((8, 8, 128), F32)

    def columns(v):
        before = jnp.where(first_col, zero, pltpu.roll(v, 1, 2))
        after = jnp.where(last_col, zero, pltpu.roll(v, 127, 2))
        return before, v, after

    def rows_down(v):
        swapped = pltpu.roll(v, WW, 2)
        above = jnp.concatenate([zero[:1], swapped[:-1]], axis=0)
        return jnp.where(first_row, above, swapped)

    def rows_up(v):
        swapped = pltpu.roll(v, WW, 2)
        below = jnp.concatenate([swapped[1:], zero[:1]], axis=0)
        return jnp.where(first_row, swapped, below)

    def conv(src, d, flip):
        @pl.loop(0, CH // 8)
        def _(g):
            rows = pl.ds(pl.multiple_of(8 * g, 8), 8)
            sums = [None] * 3
            for a in range(3):
                shifted = columns(src[pl.ds(8 * (d + a), 8), rows, :])
                for b in range(3):
                    for e in range(3):
                        tap = 9 * a + 3 * b + e
                        tap = 26 - tap if flip else tap
                        term = tb[tap, rows, :][None] * shifted[e]
                        sums[b] = term if sums[b] is None else sums[b] + term
            sp32[pl.ds(8 * d, 8), rows, :] = rows_down(sums[0]) + sums[1] + rows_up(sums[2])

    def widen(src, start, dst, chunk):
        for j in range(8):
            dst[chunk + j] = src[:, pl.ds(start + 128 * j, 128)].astype(F32)

    def pointwise(d):
        @pl.loop(0, 8)
        def _(j):
            at_chunk = 8 * d + j
            cells = lanes(128 * at_chunk, 128)
            spatial = sp32[at_chunk]
            sig = lax.logistic(spatial)
            grad = up[:, cells].astype(F32) * (sig * (1.0 + spatial * (1.0 - sig)))
            grad = grad.astype(BF16)
            sgb[:, cells] = grad
            sg32[8 + at_chunk] = grad.astype(F32)
            out[:, cells] = (vol[:, cells].astype(F32) + spatial * sig).astype(BF16)

    def forward_planes(first, step):
        @pl.loop(0, 2)
        def _(i):
            d = first + step * i
            conv(m32, d, False)
            pointwise(d)

    def backward_planes(first, step):
        @pl.loop(0, 2)
        def _(i):
            d = first + step * i
            conv(sg32, d, True)

            @pl.loop(0, 8)
            def _(j):
                mgb[:, lanes(128 * (8 * d + j), 128)] = sp32[8 * d + j].astype(BF16)

    def tap_sums():
        @pl.loop(0, CH // 8)
        def _(g):
            rows = pl.ds(pl.multiple_of(8 * g, 8), 8)
            for tap in range(27):
                tg[tap, rows, :] = zero[0]

            @pl.loop(0, PLANES)
            def _(d):
                grad = sg32[pl.ds(8 * d + 8, 8), rows, :]
                grads = (rows_up(grad), grad, rows_down(grad))
                for a in range(3):
                    shifted = columns(m32[pl.ds(8 * (d + a), 8), rows, :])
                    for b in range(3):
                        for e in range(3):
                            tap = 9 * a + 3 * b + e
                            tg[tap, rows, :] = tg[tap, rows, :] + jnp.sum(grads[b] * shifted[e], axis=0)

        tap_lane = lax.broadcasted_iota(jnp.int32, (CH, 128), 1)
        total = jnp.zeros((CH, 128), F32)
        for tap in range(27):
            total = jnp.where(tap_lane == tap, jnp.sum(tg[tap], axis=1, keepdims=True), total)
        ts[0] = total

    halo_s = [slots.take(2), slots.take(2)]
    halo_r = [slots.take(2), slots.take(2)]
    has_low, has_high = s > 0, s < NS - 1

    def halo_low(i, src, dst):
        return copy_to(src, dst, halo_s[i], halo_r[i], at(zl, x, s - 1))

    def halo_high(i, src, dst):
        return copy_to(src, dst, halo_s[i] + 1, halo_r[i] + 1, at(zl, x, s + 1))

    def m_low():
        return halo_low(0, mb.at[:, pl.ds(CELLS, CELLS)], mb.at[:, pl.ds(5 * CELLS, CELLS)])

    def m_high():
        return halo_high(0, mb.at[:, pl.ds(4 * CELLS, CELLS)], mb.at[:, pl.ds(0, CELLS)])

    def g_low():
        return halo_low(1, sgb.at[:, pl.ds(0, CELLS)], sgh.at[:, pl.ds(CELLS, CELLS)])

    def g_high():
        return halo_high(1, sgb.at[:, pl.ds(3 * CELLS, CELLS)], sgh.at[:, pl.ds(0, CELLS)])

    def halo_arrive(i, low_ref, low_at, high_ref, high_at, dst):
        @pl.when(has_low)
        def _():
            recv(low_ref.at[:, pl.ds(low_at, CELLS)], halo_r[i] + 1, at(zl, x, s - 1))
            widen(low_ref, low_at, dst, 0)

        @pl.when(s == 0)
        def _():
            for j in range(8):
                dst[j] = jnp.zeros((CH, 128), F32)

        @pl.when(has_high)
        def _():
            recv(high_ref.at[:, pl.ds(high_at, CELLS)], halo_r[i], at(zl, x, s + 1))
            widen(high_ref, high_at, dst, 40)

        @pl.when(s == NS - 1)
        def _():
            for j in range(8):
                dst[40 + j] = jnp.zeros((CH, 128), F32)

    volume_gather = Gather(vol, vol_all)
    grad_gather = Gather(mgb, mg_all)
    mixed_scatter = Scatter(mq, mb, CELLS)
    back_scatter = Scatter(bq, bb, 0)

    w1_start()
    volume_gather.start()
    for tap in range(27):
        tb[tap] = jnp.broadcast_to(taps[:, tap : tap + 1], (CH, 128))
    w2_start()
    for j in range(CHUNKS):
        volume_gather.arrive(j)
        if j == CHUNKS // 2:
            w3_start()
    w3_wait()
    columns_own = wall[:, pl.ds(x, 1), :, :].reshape(NZ * CH, C)
    for j in range(CHUNKS):
        volume_gather.finish(j)
        multiply(columns_own, vol_all, j, mq)
        mixed_scatter.start(j)
    w4_start()
    for z in (0, 1):
        mixed_scatter.wait(z)
    pl.when(has_low)(lambda: m_low().start())
    for z in (6, 7):
        mixed_scatter.wait(z)
    pl.when(has_high)(lambda: m_high().start())
    for z in (2, 3, 4, 5):
        mixed_scatter.wait(z)

    for d in range(PLANES):
        widen(mb, CELLS * (d + 1), m32, 8 * (d + 1))
    forward_planes(1, 1)
    halo_arrive(0, mb, 0, mb, 5 * CELLS, m32)
    forward_planes(0, 3)
    pl.when(has_low)(lambda: g_low().start())
    pl.when(has_high)(lambda: g_high().start())
    w5_start()

    backward_planes(1, 1)
    tap_sums()
    halo_arrive(1, sgh, 0, sgh, CELLS, sg32)
    backward_planes(0, 3)
    grad_gather.start()

    t1s, t1r = slots.take(1), slots.take(1)
    t2s, t2r = slots.take(NY), slots.take(NY)
    t3s, t3r = slots.take(1), slots.take(1)
    send(ts.at[0], tr.at[0], t1s, t1r, at(zl, x, s_c))

    def taps_y():
        recv(tr.at[0], t1r, at(zl, x, s_c))
        ts[1] = ts[0] + tr[0]
        for t in range(1, NY):
            send(ts.at[1], tr.at[1 + y], t2s + t, t2r + t, at(zl, x, space_y(t)))
        tr[1 + y] = ts[1]

    def taps_z():
        for t in range(1, NY):
            recv(tr.at[1 + rem(y + NY - t, NY)], t2r + t, at(zl, x, space_y(NY - t)))
        ts[2] = (tr[1] + tr[2]) + (tr[3] + tr[4])
        send(ts.at[2], tr.at[5], t3s, t3r, at(zl, x, s_h))

    w5_wait()
    for z in range(NZ):
        block = wall[:, :, :, pl.ds(128 * z, 128)].reshape(C, 128)
        wt[z] = block.T.reshape(NX, CH, C)

    for j in range(CHUNKS):
        grad_gather.arrive(j)
        if j == 0:
            taps_y()
    taps_z()

    d1s, d1r = slots.take(1), slots.take(1)
    d2s, d2r = slots.take(2 * NY), slots.take(2 * NY)
    d3s, d3r = slots.take(NS), slots.take(NS)
    d4s_sem, d4r_sem = slots.take(1), slots.take(1)
    own_grad = mg_all[:, pl.ds(x, 1), :, :].reshape(NZ * CH, PART)
    for i in range(4):
        part = lax.dot_general(
            own_grad, vol_all[pl.ds(2 * i, 2)].reshape(C // 4, PART),
            (((1,), (1,)), ((), ())), preferred_element_type=F32,
        )
        dw[:, :, :, pl.ds(256 * i, 256)] = part.reshape(NZ, 2, CH // 2, C // 4)
    send(dw.at[:, 1 - c], d1, d1s, d1r, at(zl, x, s_c))

    rows_own = wt[:, pl.ds(x, 1), :, :].reshape(NZ * CH, C)

    def back(j):
        grad_gather.finish(j)
        multiply(rows_own, mg_all, j, bq)
        back_scatter.start(j)

    back(0)
    recv(d1, d1r, at(zl, x, s_c))
    summed = d1[...] + dw[:, pl.ds(c, 1)].reshape(NZ, CH // 2, C)
    d1[...] = summed
    a1b[...] = summed.astype(BF16)
    for t in range(1, NY):
        for h in range(2):
            cols = lanes(128 * (4 * h + rem(y + t, NY)), 128)
            send(a1b.at[:, :, cols], d2.at[t - 1, h], d2s + 2 * t + h, d2r + 2 * t + h, at(zl, x, space_y(t)))
    for j in range(1, CHUNKS):
        back(j)
    for h in range(2):
        summed = d1[:, :, lanes(128 * (4 * h + y), 128)]
        for t in range(1, NY):
            recv(d2.at[t - 1, h], d2r + 2 * t + h, at(zl, x, space_y(NY - t)))
            summed = summed + d2[t - 1, h].astype(F32)
        a2[h] = summed
        a2b[h] = summed.astype(BF16)
    z_own = zh * NZ + zl

    def ring(t):
        z = rem(z_own + t, NS)
        return div(z, NZ), rem(z, NZ)

    for t in (8, 7, 9, 6, 10, 5, 11, 4, 12, 3, 13, 2, 14, 1, 15):
        h, z = ring(t)
        send(a2b.at[h, z], d3.at[t - 1], d3s + t, d3r + t, at(z, x, h * 8 + y * 2 + c))
    total = a2[zh, zl]
    for t in range(1, NS):
        h, z = ring(NS - t)
        recv(d3.at[t - 1], d3r + t, at(z, x, h * 8 + y * 2 + c))
        total = total + d3[t - 1].astype(F32)
    d4s[...] = total
    send(d4s, d4r, d4s_sem, d4r_sem, at(zl, x, s_c))

    for z in range(NZ):
        back_scatter.wait(z)

    @pl.loop(0, SLAB // 128)
    def _(j):
        cells = lanes(128 * j, 128)
        vgrad[:, cells] = (up[:, cells].astype(F32) + bb[:, cells].astype(F32)).astype(BF16)

    recv(tr.at[5], t3r, at(zl, x, s_h))
    tgrad[...] = ((ts[2] + tr[5]) * norm)[:, :27]
    recv(d4r, d4r_sem, at(zl, x, s_c))
    even = c == 0
    full = jnp.concatenate(
        [jnp.where(even, d4s[...], d4r[...]), jnp.where(even, d4r[...], d4s[...])], axis=0
    )
    mgrad[...] = jnp.where(even, full[:, :64], full[:, 64:]) * norm

    for cp in pending:
        cp.wait_send()
    for low, high in ((m_low, m_high), (g_low, g_high)):
        pl.when(has_low)(lambda low=low: low().wait_send())
        pl.when(has_high)(lambda high=high: high().wait_send())
    assert slots.used <= N_SEMS, slots.used


def body(volume, mixing, kernel_taps, upstream):
    norm = 1.0 / math.sqrt(PLANES * NS * CELLS)
    vmem = pl.BlockSpec(memory_space=pltpu.VMEM)
    scratch = [
        ((NZ, NX, CH, PART), BF16),
        ((NZ, NX, CH, PART), BF16),
        ((NZ, NX, CH, C), BF16),
        ((NZ, NX, CH, C), BF16),
        ((NZ, CH, PART), BF16),
        ((NZ, CH, PART), BF16),
        ((CH, 6 * CELLS), BF16),
        ((48, CH, 128), F32),
        ((48, CH, 128), F32),
        ((32, CH, 128), F32),
        ((CH, SLAB), BF16),
        ((CH, 2 * CELLS), BF16),
        ((CH, SLAB), BF16),
        ((CH, SLAB), BF16),
        ((27, CH, 128), F32),
        ((27, CH, 128), F32),
        ((3, CH, 128), F32),
        ((6, CH, 128), F32),
        ((NZ, 2, CH // 2, C), F32),
        ((NZ, CH // 2, C), F32),
        ((NZ, CH // 2, C), BF16),
        ((3, 2, NZ, CH // 2, 128), BF16),
        ((2, NZ, CH // 2, 128), F32),
        ((2, NZ, CH // 2, 128), BF16),
        ((NS - 1, CH // 2, 128), BF16),
        ((CH // 2, 128), F32),
        ((CH // 2, 128), F32),
    ]
    output, volume_grad, mixing_grad, taps_grad = pl.pallas_call(
        functools.partial(kernel, norm),
        out_shape=(
            jax.ShapeDtypeStruct((CH, SLAB), BF16),
            jax.ShapeDtypeStruct((CH, SLAB), BF16),
            jax.ShapeDtypeStruct((CH, C // NS), F32),
            jax.ShapeDtypeStruct((CH, 27), F32),
        ),
        in_specs=[vmem] * 4,
        out_specs=(vmem,) * 4,
        scratch_shapes=[pltpu.VMEM(*one) for one in scratch] + [pltpu.SemaphoreType.DMA((N_SEMS,))],
        compiler_params=pltpu.CompilerParams(collective_id=0, has_side_effects=True),
        name="conv_block",
    )(volume.reshape(CH, SLAB), upstream.reshape(CH, SLAB), mixing, kernel_taps)
    shape = (CH, PLANES, CELLS)
    return output.reshape(shape), volume_grad.reshape(shape), mixing_grad, taps_grad


def solution(mesh):
    channel_slab = P("filter", "space", None)
    return jax.shard_map(
        body,
        mesh=mesh,
        in_specs=(channel_slab, P("filter", None), P("filter", None), channel_slab),
        out_specs=(channel_slab, channel_slab, P("filter", "space"), P("filter", None)),
        check_vma=False,
    )
```

```python
import functools
import math

import jax
import jax.numpy as jnp
from jax import lax
from jax.experimental import pallas as pl
from jax.experimental.pallas import tpu as pltpu
from jax.sharding import PartitionSpec as P

F32 = jnp.float32
BF16 = jnp.bfloat16
MESH = pl.DeviceIdType.MESH

NZ, NX, NY = 8, 4, 4
NF, NS = 32, 16
CH = 32
PLANES, CELLS, WW = 4, 1024, 64
SLAB = PLANES * CELLS
PART = SLAB // NZ
C = NF * CH
CHUNKS = 4
WIDTH = PART // CHUNKS
ORDER = (4, 3, 5, 2, 6, 1, 7)


class Slots:
    def __init__(self):
        self.used = 0

    def take(self, n):
        first = self.used
        self.used += n
        return first


N_SEMS = 480


def kernel(
    norm, vol_planes, up_planes, mix, taps, out, vgrad, mgrad, tgrad,
    vol, up, vol_all, mg_all, wall, wt, mq, bq, mb, m32, sg32, sp32, sgb, sgh, mgb, bb, tb, tg, ts, tr,
    dw, d1, a1b, d2, a2, a2b, d3, d4s, d4r, sems,
):
    f = lax.axis_index("filter")
    s = lax.axis_index("space")

    def div(a, b):
        return lax.div(a, jnp.int32(b))

    def rem(a, b):
        return lax.rem(a, jnp.int32(b))

    zl, x = div(f, NX), rem(f, NX)
    zh, c = div(s, 8), rem(s, 2)
    y = div(rem(s, 8), 2)
    s_c = s + 1 - 2 * c
    s_n = rem(s + 15 + 2 * c, NS)
    s_h = rem(s + 8, NS)

    def at(zl_, x_, s_):
        return {"filter": zl_ * NX + x_, "space": s_}

    def lanes(start, size):
        return pl.ds(pl.multiple_of(start, 128), size)

    def chunk(j):
        return pl.ds(WIDTH * j, WIDTH)

    slots = Slots()
    pending = []

    def copy_to(src, dst, ss, rs, where):
        return pltpu.make_async_remote_copy(
            src_ref=src, dst_ref=dst, send_sem=sems.at[ss], recv_sem=sems.at[rs],
            device_id=where, device_id_type=MESH,
        )

    def send(src, dst, ss, rs, where):
        cp = copy_to(src, dst, ss, rs, where)
        cp.start()
        pending.append(cp)

    def recv(dst, rs, where):
        copy_to(dst, dst, rs, rs, where).wait_recv()

    barrier = pltpu.get_barrier_semaphore()
    peers = [at(rem(zl + t, NZ), x, s) for t in range(1, NZ)]
    peers += [at(rem(zl + t, NZ), x, s_h) for t in range(NZ)]
    peers += [at(zl, rem(x + t, NX), s) for t in range(1, NX)]
    peers += [at(zl, x, s_c), at(zl, x, s_n)]
    peers += [at(zl, x, zh * 8 + rem(y + t, NY) * 2 + c) for t in range(1, NY)]
    for peer in peers:
        pl.semaphore_signal(barrier, inc=1, device_id=peer, device_id_type=MESH)

    crossing = (s == 7) | (s == 8)

    @pl.when(crossing)
    def _():
        for z in range(NZ):
            pl.semaphore_signal(barrier, inc=1, device_id=at(z, x, 15 - s), device_id_type=MESH)

    for i in range(0, CH, 8):
        rows = pl.ds(i, 8)
        vol[rows] = (lambda v: v.reshape(8, SLAB))(vol_planes[rows])
        up[rows] = (lambda v: v.reshape(8, SLAB))(up_planes[rows])

    @pl.when(crossing)
    def _():
        pl.semaphore_wait(barrier, len(peers) + NZ)

    @pl.when((s < 7) | (s > 8))
    def _():
        pl.semaphore_wait(barrier, len(peers))

    class Gather:
        def __init__(self, src, dst):
            self.src, self.dst = src, dst
            self.zs, self.zr = slots.take(NZ * CHUNKS), slots.take(NZ * CHUNKS)
            self.xs, self.xr = slots.take(NX * CHUNKS), slots.take(NX * CHUNKS)

        def start(self):
            for j in range(CHUNKS):
                for t in ORDER:
                    zt = rem(zl + t, NZ)
                    send(self.src.at[:, lanes(PART * zt + WIDTH * j, WIDTH)], self.dst.at[zl, x, :, chunk(j)],
                         self.zs + NZ * j + t, self.zr + NZ * j + t, at(zt, x, s))
            self.dst[zl, x] = self.src[:, lanes(PART * zl, PART)]

        def take(self, j):
            for t in ORDER:
                zf = rem(zl + NZ - t, NZ)
                recv(self.dst.at[zf, x, :, chunk(j)], self.zr + NZ * j + t, at(zf, x, s))

        def arrive(self, j):
            self.take(j)
            part = self.dst.at[:, x, :, chunk(j)]
            for t in (2, 1, 3):
                send(part, part, self.xs + NX * j + t, self.xr + NX * j + t, at(zl, rem(x + t, NX), s))

        def finish(self, j):
            for t in (1, 3, 2):
                xf = rem(x + NX - t, NX)
                recv(self.dst.at[:, xf, :, chunk(j)], self.xr + NX * j + t, at(zl, xf, s))

    class PlaneGather(Gather):
        def piece(self, q, j):
            return copy_to(self.src.at[:, pl.ds(PART * q + WIDTH * j, WIDTH)], self.dst.at[zl, x, :, chunk(j)],
                           self.zs + NZ * j + q, self.zr + NZ * j + zl, at(q, x, s))

        def start(self, parts):
            for j in range(CHUNKS):
                for q in parts:
                    pl.when(zl != q)(lambda: self.piece(q, j).start())

        def own(self):
            self.dst[zl, x] = self.src[:, lanes(PART * zl, PART)]

        def take(self, j):
            for z in range(NZ):
                @pl.when(zl != z)
                def _():
                    recv(self.dst.at[z, x, :, chunk(j)], self.zr + NZ * j + z, at(z, x, s))

        def drain(self):
            for q in range(NZ):
                @pl.when(zl != q)
                def _():
                    for j in range(CHUNKS):
                        self.piece(q, j).wait_send()

    class Scatter:
        def __init__(self, src, dst, offset):
            self.src, self.dst, self.offset = src, dst, offset
            self.ss, self.sr = slots.take(NZ * CHUNKS), slots.take(NZ * CHUNKS)

        def place(self, z, j):
            return self.dst.at[:, lanes(self.offset + PART * z + WIDTH * j, WIDTH)]

        def start(self, j):
            for t in ORDER:
                zt = rem(zl + t, NZ)
                send(self.src.at[zt, :, chunk(j)], self.place(zl, j),
                     self.ss + NZ * j + t, self.sr + NZ * j + zl, at(zt, x, s))
            self.dst[:, lanes(self.offset + PART * zl + WIDTH * j, WIDTH)] = self.src[zl, :, chunk(j)]

        def wait(self, z):
            @pl.when(zl != z)
            def _():
                for j in range(CHUNKS):
                    recv(self.place(z, j), self.sr + NZ * j + z, at(z, x, s))

    def multiply(weights, data, j, dst):
        product = jnp.dot(weights, data[:, :, :, chunk(j)].reshape(C, WIDTH), preferred_element_type=F32)
        dst[:, :, chunk(j)] = product.astype(BF16).reshape(NZ, CH, WIDTH)

    k = c * 4 + y
    own_cols = lanes(128 * k, 128)
    side = lanes(512 * c, 512)
    other = lanes(512 * (1 - c), 512)
    w1s, w1r = slots.take(NZ), slots.take(NZ)
    w2s, w2r = slots.take(NY), slots.take(NY)
    w3s, w3r = slots.take(1), slots.take(1)
    w4s, w4r = slots.take(NX), slots.take(NX)
    w5s, w5r = slots.take(NX), slots.take(NX)

    def space_y(t):
        return zh * 8 + rem(y + t, NY) * 2 + c

    def w1_start():
        for t in ORDER:
            send(mix.at[:, own_cols], wall.at[zl, x, :, own_cols], w1s + t, w1r + t, at(rem(zl + t, NZ), x, s))
        wall[zl, x, :, own_cols] = mix[:, own_cols]

    def w2_start():
        for t in ORDER:
            zf = rem(zl + NZ - t, NZ)
            recv(wall.at[zf, x, :, own_cols], w1r + t, at(zf, x, s))
        part = wall.at[:, x, :, own_cols]
        for t in range(1, NY):
            send(part, part, w2s + t, w2r + t, at(zl, x, space_y(t)))

    def w3_start():
        for t in range(1, NY):
            cols = lanes(128 * (c * 4 + rem(y + NY - t, NY)), 128)
            recv(wall.at[:, x, :, cols], w2r + t, at(zl, x, space_y(NY - t)))
        part = wall.at[:, x, :, side]
        send(part, part, w3s, w3r, at(zl, x, s_c))

    def w3_wait():
        recv(wall.at[:, x, :, other], w3r, at(zl, x, s_c))

    def w4_start():
        part = wall.at[:, x, :, side]
        for t in range(1, NX):
            send(part, part, w4s + t, w4r + t, at(zl, rem(x + t, NX), s))

    def w5_start():
        for t in range(1, NX):
            xf = rem(x + NX - t, NX)
            part = wall.at[:, xf, :, side]
            recv(part, w4r + t, at(zl, xf, s))
            send(part, part, w5s + t, w5r + t, at(zl, x, s_c))

    def w5_wait():
        for t in range(1, NX):
            xf = rem(x + NX - t, NX)
            recv(wall.at[:, xf, :, other], w5r + t, at(zl, x, s_c))

    lane = lax.broadcasted_iota(jnp.int32, (8, 8, 128), 2)
    first_col = lax.rem(lane, WW) == 0
    last_col = lax.rem(lane, WW) == WW - 1
    first_row = lane < WW
    zero = jnp.zeros((8, 8, 128), F32)

    def columns(v):
        before = jnp.where(first_col, zero, pltpu.roll(v, 1, 2))
        after = jnp.where(last_col, zero, pltpu.roll(v, 127, 2))
        return before, v, after

    def rows_down(v):
        swapped = pltpu.roll(v, WW, 2)
        above = jnp.concatenate([zero[:1], swapped[:-1]], axis=0)
        return jnp.where(first_row, above, swapped)

    def rows_up(v):
        swapped = pltpu.roll(v, WW, 2)
        below = jnp.concatenate([swapped[1:], zero[:1]], axis=0)
        return jnp.where(first_row, swapped, below)

    def conv(src, d, flip):
        @pl.loop(0, CH // 8)
        def _(g):
            rows = pl.ds(pl.multiple_of(8 * g, 8), 8)
            sums = [None] * 3
            for a in range(3):
                shifted = columns(src[pl.ds(8 * (d + a), 8), rows, :])
                for b in range(3):
                    for e in range(3):
                        tap = 9 * a + 3 * b + e
                        tap = 26 - tap if flip else tap
                        term = tb[tap, rows, :][None] * shifted[e]
                        sums[b] = term if sums[b] is None else sums[b] + term
            sp32[pl.ds(8 * d, 8), rows, :] = rows_down(sums[0]) + sums[1] + rows_up(sums[2])

    def widen(src, start, dst, chunk):
        for j in range(8):
            dst[chunk + j] = src[:, pl.ds(start + 128 * j, 128)].astype(F32)

    def pointwise(d):
        @pl.loop(0, 8)
        def _(j):
            at_chunk = 8 * d + j
            cells = lanes(128 * at_chunk, 128)
            spatial = sp32[at_chunk]
            sig = lax.logistic(spatial)
            grad = up[:, cells].astype(F32) * (sig * (1.0 + spatial * (1.0 - sig)))
            grad = grad.astype(BF16)
            sgb[:, cells] = grad
            sg32[8 + at_chunk] = grad.astype(F32)
            out[:, cells] = (vol[:, cells].astype(F32) + spatial * sig).astype(BF16)

    def forward_planes(first, step, count):
        @pl.loop(0, count)
        def _(i):
            d = first + step * i
            conv(m32, d, False)
            pointwise(d)

    def backward_planes(first, step):
        @pl.loop(0, 2)
        def _(i):
            d = first + step * i
            conv(sg32, d, True)

            @pl.loop(0, 8)
            def _(j):
                mgb[:, lanes(128 * (8 * d + j), 128)] = sp32[8 * d + j].astype(BF16)

    def tap_sums():
        @pl.loop(0, CH // 8)
        def _(g):
            rows = pl.ds(pl.multiple_of(8 * g, 8), 8)
            for tap in range(27):
                tg[tap, rows, :] = zero[0]

            @pl.loop(0, PLANES)
            def _(d):
                grad = sg32[pl.ds(8 * d + 8, 8), rows, :]
                grads = (rows_up(grad), grad, rows_down(grad))
                for a in range(3):
                    shifted = columns(m32[pl.ds(8 * (d + a), 8), rows, :])
                    for b in range(3):
                        for e in range(3):
                            tap = 9 * a + 3 * b + e
                            tg[tap, rows, :] = tg[tap, rows, :] + jnp.sum(grads[b] * shifted[e], axis=0)

        tap_lane = lax.broadcasted_iota(jnp.int32, (CH, 128), 1)
        total = jnp.zeros((CH, 128), F32)
        for tap in range(27):
            total = jnp.where(tap_lane == tap, jnp.sum(tg[tap], axis=1, keepdims=True), total)
        ts[0] = total

    halo_s = [slots.take(2), slots.take(2)]
    halo_r = [slots.take(2), slots.take(2)]
    has_low, has_high = s > 0, s < NS - 1
    sends_low, sends_high = (s > 0) & (s != 8), (s < NS - 1) & (s != 7)

    def halo_low(i, src, dst):
        return copy_to(src, dst, halo_s[i], halo_r[i], at(zl, x, s - 1))

    def halo_high(i, src, dst):
        return copy_to(src, dst, halo_s[i] + 1, halo_r[i] + 1, at(zl, x, s + 1))

    def m_low():
        return halo_low(0, mb.at[:, pl.ds(CELLS, CELLS)], mb.at[:, pl.ds(5 * CELLS, CELLS)])

    def m_high():
        return halo_high(0, mb.at[:, pl.ds(4 * CELLS, CELLS)], mb.at[:, pl.ds(0, CELLS)])

    def g_low():
        return halo_low(1, sgb.at[:, pl.ds(0, CELLS)], sgh.at[:, pl.ds(CELLS, CELLS)])

    def g_high():
        return halo_high(1, sgb.at[:, pl.ds(3 * CELLS, CELLS)], sgh.at[:, pl.ds(0, CELLS)])

    cross_s, cross_r = slots.take(NZ * CHUNKS), slots.take(2 * CHUNKS)
    cross_part = zl - 6 * (8 - s)
    cross_sends = ((s == 7) & (zl >= 6)) | ((s == 8) & (zl <= 1))

    def cross_copy(z, j):
        place = mb.at[:, lanes(5 * CELLS * (s - 7) + PART * cross_part + WIDTH * j, WIDTH)]
        return copy_to(mq.at[z, :, chunk(j)], place, cross_s + NZ * j + z,
                       cross_r + CHUNKS * cross_part + j, at(z, x, 15 - s))

    def cross_start(j):
        @pl.when(cross_sends)
        def _():
            for z in range(NZ):
                cross_copy(z, j).start()

    def cross_arrive(start, first_z):
        for part in range(2):
            for j in range(CHUNKS):
                recv(mb.at[:, pl.ds(start + PART * part + WIDTH * j, WIDTH)],
                     cross_r + CHUNKS * part + j, at(first_z + part, x, 15 - s))

    def mixed_halo_arrive():
        @pl.when((s > 0) & (s != 8))
        def _():
            recv(mb.at[:, pl.ds(0, CELLS)], halo_r[0] + 1, at(zl, x, s - 1))

        pl.when(s == 8)(lambda: cross_arrive(0, 6))

        @pl.when((s < NS - 1) & (s != 7))
        def _():
            recv(mb.at[:, pl.ds(5 * CELLS, CELLS)], halo_r[0], at(zl, x, s + 1))

        pl.when(s == 7)(lambda: cross_arrive(5 * CELLS, 0))
        for edge, start, row in ((s == 0, 0, 0), (s == NS - 1, 5 * CELLS, 40)):
            @pl.when(edge)
            def _():
                for j in range(8):
                    m32[row + j] = jnp.zeros((CH, 128), F32)

            @pl.when(jnp.logical_not(edge))
            def _():
                widen(mb, start, m32, row)

    def halo_arrive(i, low_ref, low_at, high_ref, high_at, dst):
        @pl.when(has_low)
        def _():
            recv(low_ref.at[:, pl.ds(low_at, CELLS)], halo_r[i] + 1, at(zl, x, s - 1))
            widen(low_ref, low_at, dst, 0)

        @pl.when(s == 0)
        def _():
            for j in range(8):
                dst[j] = jnp.zeros((CH, 128), F32)

        @pl.when(has_high)
        def _():
            recv(high_ref.at[:, pl.ds(high_at, CELLS)], halo_r[i], at(zl, x, s + 1))
            widen(high_ref, high_at, dst, 40)

        @pl.when(s == NS - 1)
        def _():
            for j in range(8):
                dst[40 + j] = jnp.zeros((CH, 128), F32)

    volume_gather = Gather(vol, vol_all)
    grad_gather = PlaneGather(mgb, mg_all)
    mixed_scatter = Scatter(mq, mb, CELLS)
    back_scatter = Scatter(bq, bb, 0)

    w1_start()
    volume_gather.start()
    for tap in range(27):
        tb[tap] = jnp.broadcast_to(taps[:, tap : tap + 1], (CH, 128))
    w2_start()
    for j in range(CHUNKS):
        volume_gather.arrive(j)
        if j == CHUNKS // 2:
            w3_start()
    w3_wait()
    columns_own = wall[:, pl.ds(x, 1), :, :].reshape(NZ * CH, C)
    for j in range(CHUNKS):
        volume_gather.finish(j)
        multiply(columns_own, vol_all, j, mq)
        mixed_scatter.start(j)
        cross_start(j)
    w4_start()
    for z in (0, 1):
        mixed_scatter.wait(z)
    pl.when(sends_low)(lambda: m_low().start())
    for z in (6, 7):
        mixed_scatter.wait(z)
    pl.when(sends_high)(lambda: m_high().start())
    for z in (2, 3, 4, 5):
        mixed_scatter.wait(z)

    for d in range(PLANES):
        widen(mb, CELLS * (d + 1), m32, 8 * (d + 1))
    forward_planes(1, 1, 1)
    mixed_halo_arrive()
    forward_planes(0, 3, 2)
    pl.when(has_low)(lambda: g_low().start())
    pl.when(has_high)(lambda: g_high().start())
    w5_start()

    forward_planes(2, 1, 1)
    backward_planes(1, 1)
    grad_gather.start((3, 4, 2, 5))
    tap_sums()
    halo_arrive(1, sgh, 0, sgh, CELLS, sg32)
    backward_planes(0, 3)
    grad_gather.start((0, 7, 1, 6))
    grad_gather.own()

    t1s, t1r = slots.take(1), slots.take(1)
    t2s, t2r = slots.take(NY), slots.take(NY)
    t3s, t3r = slots.take(1), slots.take(1)
    send(ts.at[0], tr.at[0], t1s, t1r, at(zl, x, s_c))

    def taps_y():
        recv(tr.at[0], t1r, at(zl, x, s_c))
        ts[1] = ts[0] + tr[0]
        for t in range(1, NY):
            send(ts.at[1], tr.at[1 + y], t2s + t, t2r + t, at(zl, x, space_y(t)))
        tr[1 + y] = ts[1]

    def taps_z():
        for t in range(1, NY):
            recv(tr.at[1 + rem(y + NY - t, NY)], t2r + t, at(zl, x, space_y(NY - t)))
        ts[2] = (tr[1] + tr[2]) + (tr[3] + tr[4])
        send(ts.at[2], tr.at[5], t3s, t3r, at(zl, x, s_h))

    w5_wait()
    for z in range(NZ):
        block = wall[:, :, :, pl.ds(128 * z, 128)].reshape(C, 128)
        wt[z] = block.T.reshape(NX, CH, C)

    for j in range(CHUNKS):
        grad_gather.arrive(j)
        if j == 0:
            taps_y()
    taps_z()

    d1s, d1r = slots.take(1), slots.take(1)
    d2s, d2r = slots.take(2 * NY), slots.take(2 * NY)
    d3s, d3r = slots.take(NS), slots.take(NS)
    d4s_sem, d4r_sem = slots.take(1), slots.take(1)
    own_grad = mg_all[:, pl.ds(x, 1), :, :].reshape(NZ * CH, PART)
    for i in range(4):
        part = lax.dot_general(
            own_grad, vol_all[pl.ds(2 * i, 2)].reshape(C // 4, PART),
            (((1,), (1,)), ((), ())), preferred_element_type=F32,
        )
        dw[:, :, :, pl.ds(256 * i, 256)] = part.reshape(NZ, 2, CH // 2, C // 4)
    send(dw.at[:, 1 - c], d1, d1s, d1r, at(zl, x, s_c))

    rows_own = wt[:, pl.ds(x, 1), :, :].reshape(NZ * CH, C)

    def back(j):
        grad_gather.finish(j)
        multiply(rows_own, mg_all, j, bq)
        back_scatter.start(j)

    back(0)
    recv(d1, d1r, at(zl, x, s_c))
    summed = d1[...] + dw[:, pl.ds(c, 1)].reshape(NZ, CH // 2, C)
    d1[...] = summed
    a1b[...] = summed.astype(BF16)
    for t in range(1, NY):
        for h in range(2):
            cols = lanes(128 * (4 * h + rem(y + t, NY)), 128)
            send(a1b.at[:, :, cols], d2.at[t - 1, h], d2s + 2 * t + h, d2r + 2 * t + h, at(zl, x, space_y(t)))
    for j in range(1, CHUNKS):
        back(j)
    for h in range(2):
        summed = d1[:, :, lanes(128 * (4 * h + y), 128)]
        for t in range(1, NY):
            recv(d2.at[t - 1, h], d2r + 2 * t + h, at(zl, x, space_y(NY - t)))
            summed = summed + d2[t - 1, h].astype(F32)
        a2[h] = summed
        a2b[h] = summed.astype(BF16)
    z_own = zh * NZ + zl

    def ring(t):
        z = rem(z_own + t, NS)
        return div(z, NZ), rem(z, NZ)

    for t in (8, 7, 9, 6, 10, 5, 11, 4, 12, 3, 13, 2, 14, 1, 15):
        h, z = ring(t)
        send(a2b.at[h, z], d3.at[t - 1], d3s + t, d3r + t, at(z, x, h * 8 + y * 2 + c))
    total = a2[zh, zl]
    for t in range(1, NS):
        h, z = ring(NS - t)
        recv(d3.at[t - 1], d3r + t, at(z, x, h * 8 + y * 2 + c))
        total = total + d3[t - 1].astype(F32)
    d4s[...] = total
    send(d4s, d4r, d4s_sem, d4r_sem, at(zl, x, s_c))

    for z in range(NZ):
        back_scatter.wait(z)

    @pl.loop(0, SLAB // 128)
    def _(j):
        cells = lanes(128 * j, 128)
        vgrad[:, cells] = (up[:, cells].astype(F32) + bb[:, cells].astype(F32)).astype(BF16)

    recv(tr.at[5], t3r, at(zl, x, s_h))
    tgrad[...] = ((ts[2] + tr[5]) * norm)[:, :27]
    recv(d4r, d4r_sem, at(zl, x, s_c))
    even = c == 0
    full = jnp.concatenate(
        [jnp.where(even, d4s[...], d4r[...]), jnp.where(even, d4r[...], d4s[...])], axis=0
    )
    mgrad[...] = jnp.where(even, full[:, :64], full[:, 64:]) * norm

    for cp in pending:
        cp.wait_send()
    pl.when(sends_low)(lambda: m_low().wait_send())
    pl.when(sends_high)(lambda: m_high().wait_send())
    pl.when(has_low)(lambda: g_low().wait_send())
    pl.when(has_high)(lambda: g_high().wait_send())
    grad_gather.drain()

    @pl.when(cross_sends)
    def _():
        for j in range(CHUNKS):
            for z in range(NZ):
                cross_copy(z, j).wait_send()

    assert slots.used <= N_SEMS, slots.used


def body(volume, mixing, kernel_taps, upstream):
    norm = 1.0 / math.sqrt(PLANES * NS * CELLS)
    vmem = pl.BlockSpec(memory_space=pltpu.VMEM)
    scratch = [
        ((CH, SLAB), BF16),
        ((CH, SLAB), BF16),
        ((NZ, NX, CH, PART), BF16),
        ((NZ, NX, CH, PART), BF16),
        ((NZ, NX, CH, C), BF16),
        ((NZ, NX, CH, C), BF16),
        ((NZ, CH, PART), BF16),
        ((NZ, CH, PART), BF16),
        ((CH, 6 * CELLS), BF16),
        ((48, CH, 128), F32),
        ((48, CH, 128), F32),
        ((32, CH, 128), F32),
        ((CH, SLAB), BF16),
        ((CH, 2 * CELLS), BF16),
        ((CH, SLAB), BF16),
        ((CH, SLAB), BF16),
        ((27, CH, 128), F32),
        ((27, CH, 128), F32),
        ((3, CH, 128), F32),
        ((6, CH, 128), F32),
        ((NZ, 2, CH // 2, C), F32),
        ((NZ, CH // 2, C), F32),
        ((NZ, CH // 2, C), BF16),
        ((3, 2, NZ, CH // 2, 128), BF16),
        ((2, NZ, CH // 2, 128), F32),
        ((2, NZ, CH // 2, 128), BF16),
        ((NS - 1, CH // 2, 128), BF16),
        ((CH // 2, 128), F32),
        ((CH // 2, 128), F32),
    ]
    output, volume_grad, mixing_grad, taps_grad = pl.pallas_call(
        functools.partial(kernel, norm),
        out_shape=(
            jax.ShapeDtypeStruct((CH, SLAB), BF16),
            jax.ShapeDtypeStruct((CH, SLAB), BF16),
            jax.ShapeDtypeStruct((CH, C // NS), F32),
            jax.ShapeDtypeStruct((CH, 27), F32),
        ),
        in_specs=[vmem] * 4,
        out_specs=(vmem,) * 4,
        scratch_shapes=[pltpu.VMEM(*one) for one in scratch] + [pltpu.SemaphoreType.DMA((N_SEMS,))],
        compiler_params=pltpu.CompilerParams(collective_id=0, has_side_effects=True),
        name="conv_block",
    )(volume, upstream, mixing, kernel_taps)

    def finish(o_ref, v_ref, m_ref, t_ref, out, vgrad, mgrad, tgrad):
        for i in range(0, CH, 8):
            rows = pl.ds(i, 8)
            out[rows] = (lambda v: v.reshape(8, PLANES, CELLS))(o_ref[rows])
            vgrad[rows] = (lambda v: v.reshape(8, PLANES, CELLS))(v_ref[rows])
        mgrad[...] = m_ref[...]
        tgrad[...] = t_ref[...]

    return pl.pallas_call(
        finish,
        out_shape=(
            jax.ShapeDtypeStruct((CH, PLANES, CELLS), BF16),
            jax.ShapeDtypeStruct((CH, PLANES, CELLS), BF16),
            jax.ShapeDtypeStruct((CH, C // NS), F32),
            jax.ShapeDtypeStruct((CH, 27), F32),
        ),
        in_specs=[vmem] * 4,
        out_specs=(vmem,) * 4,
        name="by_planes",
    )(output, volume_grad, mixing_grad, taps_grad)


def solution(mesh):
    channel_slab = P("filter", "space", None)
    return jax.shard_map(
        body,
        mesh=mesh,
        in_specs=(channel_slab, P("filter", None), P("filter", None), channel_slab),
        out_specs=(channel_slab, channel_slab, P("filter", "space"), P("filter", None)),
        check_vma=False,
    )
```

```python
import functools
import math

import jax
import jax.numpy as jnp
from jax import lax
from jax.experimental import pallas as pl
from jax.experimental.pallas import tpu as pltpu
from jax.sharding import PartitionSpec as P

F32 = jnp.float32
BF16 = jnp.bfloat16
MESH = pl.DeviceIdType.MESH

NZ, NX, NY = 8, 4, 4
NF, NS = 32, 16
CH = 32
PLANES, CELLS, WW = 4, 1024, 64
SLAB = PLANES * CELLS
PART = SLAB // NZ
C = NF * CH
CHUNKS = 4
WIDTH = PART // CHUNKS
ORDER = (4, 3, 5, 2, 6, 1, 7)


class Slots:
    def __init__(self):
        self.used = 0

    def take(self, n):
        first = self.used
        self.used += n
        return first


N_SEMS = 480


def kernel(
    norm, vol_planes, up_planes, mix, taps, out, vgrad, mgrad, tgrad,
    vol, up, vol_all, mg_all, wall, wt, mq, bq, mb, m32, sg32, sp32, sgb, sgh, mgb, bb, tb, tg, ts, tr,
    dw, dwb, d1, d1b, a1b, d2, a2, a2b, d3, d4s, d4r, sems, token,
):
    f = lax.axis_index("filter")
    s = lax.axis_index("space")

    def div(a, b):
        return lax.div(a, jnp.int32(b))

    def rem(a, b):
        return lax.rem(a, jnp.int32(b))

    zl, x = div(f, NX), rem(f, NX)
    zh, c = div(s, 8), rem(s, 2)
    y = div(rem(s, 8), 2)
    s_c = s + 1 - 2 * c
    s_n = zh * 8 + rem(rem(s, 8) + 7 + 2 * c, 8)
    s_h = rem(s + 8, NS)

    def at(zl_, x_, s_):
        return {"filter": zl_ * NX + x_, "space": s_}

    def lanes(start, size):
        return pl.ds(pl.multiple_of(start, 128), size)

    def chunk(j):
        return pl.ds(WIDTH * j, WIDTH)

    slots = Slots()
    pending = []

    def copy_to(src, dst, ss, rs, where):
        return pltpu.make_async_remote_copy(
            src_ref=src, dst_ref=dst, send_sem=sems.at[ss], recv_sem=sems.at[rs],
            device_id=where, device_id_type=MESH,
        )

    def send(src, dst, ss, rs, where):
        cp = copy_to(src, dst, ss, rs, where)
        cp.start()
        pending.append(cp)

    def recv(dst, rs, where):
        copy_to(dst, dst, rs, rs, where).wait_recv()

    barrier = pltpu.get_barrier_semaphore()
    peers = [at(rem(zl + t, NZ), x, s) for t in range(1, NZ)]
    peers += [at(zl, rem(x + t, NX), s) for t in range(1, NX)]
    peers += [at(zl, x, s_c), at(zl, x, s_n)]
    peers += [at(zl, x, zh * 8 + rem(y + t, NY) * 2 + c) for t in range(1, NY)]
    for peer in peers:
        pl.semaphore_signal(barrier, inc=1, device_id=peer, device_id_type=MESH)

    edge = ((zl == 0) & (zh == 0)) | ((zl == NZ - 1) & (zh == 1))
    partner = at(NZ - 1 - zl, x, s_h)

    @pl.when(edge)
    def _():
        pl.semaphore_signal(barrier, inc=1, device_id=partner, device_id_type=MESH)

    for i in range(0, CH, 8):
        rows = pl.ds(i, 8)
        vol[rows] = (lambda v: v.reshape(8, SLAB))(vol_planes[rows])
        up[rows] = (lambda v: v.reshape(8, SLAB))(up_planes[rows])

    def tell(i, where):
        pl.semaphore_signal(token.at[i], inc=1, device_id=where, device_id_type=MESH)

    @pl.when(edge)
    def _():
        pl.semaphore_wait(barrier, len(peers) + 1)
        tell(0, partner)

    @pl.when(jnp.logical_not(edge))
    def _():
        pl.semaphore_wait(barrier, len(peers))

    def other_half_to_column():
        @pl.when(edge)
        def _():
            pl.semaphore_wait(token.at[0], 1)
            for t in range(1, NZ):
                tell(0, at(rem(zl + t, NZ), x, s))

    def other_half_known():
        pl.when(jnp.logical_not(edge))(lambda: pl.semaphore_wait(token.at[0], 1))
        pl.when(s == 0)(lambda: tell(1, at(zl, x, 7)))
        pl.when(s == NS - 1)(lambda: tell(1, at(zl, x, 8)))
        pl.when((s == 7) | (s == 8))(lambda: pl.semaphore_wait(token.at[1], 1))

    class Gather:
        def __init__(self, src, dst):
            self.src, self.dst = src, dst
            self.zs, self.zr = slots.take(NZ * CHUNKS), slots.take(NZ * CHUNKS)
            self.xs, self.xr = slots.take(NX * CHUNKS), slots.take(NX * CHUNKS)

        def start(self):
            for j in range(CHUNKS):
                for t in ORDER:
                    zt = rem(zl + t, NZ)
                    send(self.src.at[:, lanes(PART * zt + WIDTH * j, WIDTH)], self.dst.at[zl, x, :, chunk(j)],
                         self.zs + NZ * j + t, self.zr + NZ * j + t, at(zt, x, s))
            self.dst[zl, x] = self.src[:, lanes(PART * zl, PART)]

        def take(self, j):
            for t in ORDER:
                zf = rem(zl + NZ - t, NZ)
                recv(self.dst.at[zf, x, :, chunk(j)], self.zr + NZ * j + t, at(zf, x, s))

        def arrive(self, j):
            self.take(j)
            part = self.dst.at[:, x, :, chunk(j)]
            for t in (2, 1, 3):
                send(part, part, self.xs + NX * j + t, self.xr + NX * j + t, at(zl, rem(x + t, NX), s))

        def finish(self, j):
            for t in (1, 3, 2):
                xf = rem(x + NX - t, NX)
                recv(self.dst.at[:, xf, :, chunk(j)], self.xr + NX * j + t, at(zl, xf, s))

    class PlaneGather(Gather):
        def piece(self, q, j):
            return copy_to(self.src.at[:, pl.ds(PART * q + WIDTH * j, WIDTH)], self.dst.at[zl, x, :, chunk(j)],
                           self.zs + NZ * j + q, self.zr + NZ * j + zl, at(q, x, s))

        def start(self, parts):
            for j in range(CHUNKS):
                for q in parts:
                    pl.when(zl != q)(lambda: self.piece(q, j).start())

        def own(self):
            self.dst[zl, x] = self.src[:, lanes(PART * zl, PART)]

        def take(self, j):
            for z in range(NZ):
                @pl.when(zl != z)
                def _():
                    recv(self.dst.at[z, x, :, chunk(j)], self.zr + NZ * j + z, at(z, x, s))

        def drain(self):
            for q in range(NZ):
                @pl.when(zl != q)
                def _():
                    for j in range(CHUNKS):
                        self.piece(q, j).wait_send()

    class Scatter:
        def __init__(self, src, dst, offset):
            self.src, self.dst, self.offset = src, dst, offset
            self.ss, self.sr = slots.take(NZ * CHUNKS), slots.take(NZ * CHUNKS)

        def place(self, z, j):
            return self.dst.at[:, lanes(self.offset + PART * z + WIDTH * j, WIDTH)]

        def start(self, j):
            for t in ORDER:
                zt = rem(zl + t, NZ)
                send(self.src.at[zt, :, chunk(j)], self.place(zl, j),
                     self.ss + NZ * j + t, self.sr + NZ * j + zl, at(zt, x, s))
            self.dst[:, lanes(self.offset + PART * zl + WIDTH * j, WIDTH)] = self.src[zl, :, chunk(j)]

        def wait(self, z):
            @pl.when(zl != z)
            def _():
                for j in range(CHUNKS):
                    recv(self.place(z, j), self.sr + NZ * j + z, at(z, x, s))

    def multiply(weights, data, j, dst):
        product = jnp.dot(weights, data[:, :, :, chunk(j)].reshape(C, WIDTH), preferred_element_type=F32)
        dst[:, :, chunk(j)] = product.astype(BF16).reshape(NZ, CH, WIDTH)

    k = c * 4 + y
    own_cols = lanes(128 * k, 128)
    side = lanes(512 * c, 512)
    other = lanes(512 * (1 - c), 512)
    w1s, w1r = slots.take(NZ), slots.take(NZ)
    w2s, w2r = slots.take(NY), slots.take(NY)
    w3s, w3r = slots.take(1), slots.take(1)
    w4s, w4r = slots.take(NX), slots.take(NX)
    w5s, w5r = slots.take(NX), slots.take(NX)

    def space_y(t):
        return zh * 8 + rem(y + t, NY) * 2 + c

    def w1_start():
        for t in ORDER:
            send(mix.at[:, own_cols], wall.at[zl, x, :, own_cols], w1s + t, w1r + t, at(rem(zl + t, NZ), x, s))
        wall[zl, x, :, own_cols] = mix[:, own_cols]

    def w2_start():
        for t in ORDER:
            zf = rem(zl + NZ - t, NZ)
            recv(wall.at[zf, x, :, own_cols], w1r + t, at(zf, x, s))
        part = wall.at[:, x, :, own_cols]
        for t in range(1, NY):
            send(part, part, w2s + t, w2r + t, at(zl, x, space_y(t)))

    def w3_start():
        for t in range(1, NY):
            cols = lanes(128 * (c * 4 + rem(y + NY - t, NY)), 128)
            recv(wall.at[:, x, :, cols], w2r + t, at(zl, x, space_y(NY - t)))
        part = wall.at[:, x, :, side]
        send(part, part, w3s, w3r, at(zl, x, s_c))

    def w3_wait():
        recv(wall.at[:, x, :, other], w3r, at(zl, x, s_c))

    def w4_start():
        part = wall.at[:, x, :, side]
        for t in range(1, NX):
            send(part, part, w4s + t, w4r + t, at(zl, rem(x + t, NX), s))

    def w5_start():
        for t in range(1, NX):
            xf = rem(x + NX - t, NX)
            part = wall.at[:, xf, :, side]
            recv(part, w4r + t, at(zl, xf, s))
            send(part, part, w5s + t, w5r + t, at(zl, x, s_c))

    def w5_wait():
        for t in range(1, NX):
            xf = rem(x + NX - t, NX)
            recv(wall.at[:, xf, :, other], w5r + t, at(zl, x, s_c))

    lane = lax.broadcasted_iota(jnp.int32, (8, 8, 128), 2)
    first_col = lax.rem(lane, WW) == 0
    last_col = lax.rem(lane, WW) == WW - 1
    first_row = lane < WW
    zero = jnp.zeros((8, 8, 128), F32)

    def columns(v):
        before = jnp.where(first_col, zero, pltpu.roll(v, 1, 2))
        after = jnp.where(last_col, zero, pltpu.roll(v, 127, 2))
        return before, v, after

    def rows_down(v):
        swapped = pltpu.roll(v, WW, 2)
        above = jnp.concatenate([zero[:1], swapped[:-1]], axis=0)
        return jnp.where(first_row, above, swapped)

    def rows_up(v):
        swapped = pltpu.roll(v, WW, 2)
        below = jnp.concatenate([swapped[1:], zero[:1]], axis=0)
        return jnp.where(first_row, swapped, below)

    def conv(src, d, flip):
        @pl.loop(0, CH // 8)
        def _(g):
            rows = pl.ds(pl.multiple_of(8 * g, 8), 8)
            sums = [None] * 3
            for a in range(3):
                shifted = columns(src[pl.ds(8 * (d + a), 8), rows, :])
                for b in range(3):
                    for e in range(3):
                        tap = 9 * a + 3 * b + e
                        tap = 26 - tap if flip else tap
                        term = tb[tap, rows, :][None] * shifted[e]
                        sums[b] = term if sums[b] is None else sums[b] + term
            sp32[pl.ds(8 * d, 8), rows, :] = rows_down(sums[0]) + sums[1] + rows_up(sums[2])

    def widen(src, start, dst, chunk):
        for j in range(8):
            dst[chunk + j] = src[:, pl.ds(start + 128 * j, 128)].astype(F32)

    def pointwise(d):
        @pl.loop(0, 8)
        def _(j):
            at_chunk = 8 * d + j
            cells = lanes(128 * at_chunk, 128)
            spatial = sp32[at_chunk]
            sig = lax.logistic(spatial)
            grad = up[:, cells].astype(F32) * (sig * (1.0 + spatial * (1.0 - sig)))
            grad = grad.astype(BF16)
            sgb[:, cells] = grad
            sg32[8 + at_chunk] = grad.astype(F32)
            out[:, cells] = (vol[:, cells].astype(F32) + spatial * sig).astype(BF16)

    def forward_planes(first, step, count):
        @pl.loop(0, count)
        def _(i):
            d = first + step * i
            conv(m32, d, False)
            pointwise(d)

    def backward_planes(first, step):
        @pl.loop(0, 2)
        def _(i):
            d = first + step * i
            conv(sg32, d, True)

            @pl.loop(0, 8)
            def _(j):
                mgb[:, lanes(128 * (8 * d + j), 128)] = sp32[8 * d + j].astype(BF16)

    def tap_sums():
        @pl.loop(0, CH // 8)
        def _(g):
            rows = pl.ds(pl.multiple_of(8 * g, 8), 8)
            for tap in range(27):
                tg[tap, rows, :] = zero[0]

            @pl.loop(0, PLANES)
            def _(d):
                grad = sg32[pl.ds(8 * d + 8, 8), rows, :]
                grads = (rows_up(grad), grad, rows_down(grad))
                for a in range(3):
                    shifted = columns(m32[pl.ds(8 * (d + a), 8), rows, :])
                    for b in range(3):
                        for e in range(3):
                            tap = 9 * a + 3 * b + e
                            tg[tap, rows, :] = tg[tap, rows, :] + jnp.sum(grads[b] * shifted[e], axis=0)

        tap_lane = lax.broadcasted_iota(jnp.int32, (CH, 128), 1)
        total = jnp.zeros((CH, 128), F32)
        for tap in range(27):
            total = jnp.where(tap_lane == tap, jnp.sum(tg[tap], axis=1, keepdims=True), total)
        ts[0] = total

    halo_s = [slots.take(2), slots.take(2)]
    halo_r = [slots.take(2), slots.take(2)]
    has_low, has_high = s > 0, s < NS - 1
    sends_low, sends_high = (s > 0) & (s != 8), (s < NS - 1) & (s != 7)

    def halo_low(i, src, dst):
        return copy_to(src, dst, halo_s[i], halo_r[i], at(zl, x, s - 1))

    def halo_high(i, src, dst):
        return copy_to(src, dst, halo_s[i] + 1, halo_r[i] + 1, at(zl, x, s + 1))

    def m_low():
        return halo_low(0, mb.at[:, pl.ds(CELLS, CELLS)], mb.at[:, pl.ds(5 * CELLS, CELLS)])

    def m_high():
        return halo_high(0, mb.at[:, pl.ds(4 * CELLS, CELLS)], mb.at[:, pl.ds(0, CELLS)])

    def g_low():
        return halo_low(1, sgb.at[:, pl.ds(0, CELLS)], sgh.at[:, pl.ds(CELLS, CELLS)])

    def g_high():
        return halo_high(1, sgb.at[:, pl.ds(3 * CELLS, CELLS)], sgh.at[:, pl.ds(0, CELLS)])

    cross_s, cross_r = slots.take(NZ * CHUNKS), slots.take(2 * CHUNKS)
    cross_part = zl - 6 * (8 - s)
    cross_sends = ((s == 7) & (zl >= 6)) | ((s == 8) & (zl <= 1))

    def cross_copy(z, j):
        place = mb.at[:, lanes(5 * CELLS * (s - 7) + PART * cross_part + WIDTH * j, WIDTH)]
        return copy_to(mq.at[z, :, chunk(j)], place, cross_s + NZ * j + z,
                       cross_r + CHUNKS * cross_part + j, at(z, x, 15 - s))

    def cross_start(j):
        @pl.when(cross_sends)
        def _():
            for z in range(NZ):
                cross_copy(z, j).start()

    def cross_arrive(start, first_z):
        for part in range(2):
            for j in range(CHUNKS):
                recv(mb.at[:, pl.ds(start + PART * part + WIDTH * j, WIDTH)],
                     cross_r + CHUNKS * part + j, at(first_z + part, x, 15 - s))

    def mixed_halo_arrive():
        @pl.when((s > 0) & (s != 8))
        def _():
            recv(mb.at[:, pl.ds(0, CELLS)], halo_r[0] + 1, at(zl, x, s - 1))

        pl.when(s == 8)(lambda: cross_arrive(0, 6))

        @pl.when((s < NS - 1) & (s != 7))
        def _():
            recv(mb.at[:, pl.ds(5 * CELLS, CELLS)], halo_r[0], at(zl, x, s + 1))

        pl.when(s == 7)(lambda: cross_arrive(5 * CELLS, 0))
        for edge, start, row in ((s == 0, 0, 0), (s == NS - 1, 5 * CELLS, 40)):
            @pl.when(edge)
            def _():
                for j in range(8):
                    m32[row + j] = jnp.zeros((CH, 128), F32)

            @pl.when(jnp.logical_not(edge))
            def _():
                widen(mb, start, m32, row)

    def halo_arrive(i, low_ref, low_at, high_ref, high_at, dst):
        @pl.when(has_low)
        def _():
            recv(low_ref.at[:, pl.ds(low_at, CELLS)], halo_r[i] + 1, at(zl, x, s - 1))
            widen(low_ref, low_at, dst, 0)

        @pl.when(s == 0)
        def _():
            for j in range(8):
                dst[j] = jnp.zeros((CH, 128), F32)

        @pl.when(has_high)
        def _():
            recv(high_ref.at[:, pl.ds(high_at, CELLS)], halo_r[i], at(zl, x, s + 1))
            widen(high_ref, high_at, dst, 40)

        @pl.when(s == NS - 1)
        def _():
            for j in range(8):
                dst[40 + j] = jnp.zeros((CH, 128), F32)

    volume_gather = Gather(vol, vol_all)
    grad_gather = PlaneGather(mgb, mg_all)
    mixed_scatter = Scatter(mq, mb, CELLS)
    back_scatter = Scatter(bq, bb, 0)

    w1_start()
    volume_gather.start()
    for tap in range(27):
        tb[tap] = jnp.broadcast_to(taps[:, tap : tap + 1], (CH, 128))
    w2_start()
    other_half_to_column()
    for j in range(CHUNKS):
        volume_gather.arrive(j)
        if j == CHUNKS // 2:
            w3_start()
    w3_wait()
    columns_own = wall[:, pl.ds(x, 1), :, :].reshape(NZ * CH, C)
    for j in range(CHUNKS):
        volume_gather.finish(j)
        multiply(columns_own, vol_all, j, mq)
        mixed_scatter.start(j)
        if j == 0:
            other_half_known()
        cross_start(j)
    w4_start()
    for z in (0, 1):
        mixed_scatter.wait(z)
    pl.when(sends_low)(lambda: m_low().start())
    for z in (6, 7):
        mixed_scatter.wait(z)
    pl.when(sends_high)(lambda: m_high().start())
    for z in (2, 3, 4, 5):
        mixed_scatter.wait(z)

    for d in range(PLANES):
        widen(mb, CELLS * (d + 1), m32, 8 * (d + 1))
    forward_planes(1, 1, 1)
    mixed_halo_arrive()
    forward_planes(0, 3, 2)
    pl.when(has_low)(lambda: g_low().start())
    pl.when(has_high)(lambda: g_high().start())
    w5_start()

    forward_planes(2, 1, 1)
    backward_planes(1, 1)
    grad_gather.start((3, 4, 2, 5))
    tap_sums()
    halo_arrive(1, sgh, 0, sgh, CELLS, sg32)
    backward_planes(0, 3)
    grad_gather.start((0, 7, 1, 6))
    grad_gather.own()

    t1s, t1r = slots.take(1), slots.take(1)
    t2s, t2r = slots.take(NY), slots.take(NY)
    t3s, t3r = slots.take(1), slots.take(1)
    send(ts.at[0], tr.at[0], t1s, t1r, at(zl, x, s_c))

    def taps_y():
        recv(tr.at[0], t1r, at(zl, x, s_c))
        ts[1] = ts[0] + tr[0]
        for t in range(1, NY):
            send(ts.at[1], tr.at[1 + y], t2s + t, t2r + t, at(zl, x, space_y(t)))
        tr[1 + y] = ts[1]

    def taps_z():
        for t in range(1, NY):
            recv(tr.at[1 + rem(y + NY - t, NY)], t2r + t, at(zl, x, space_y(NY - t)))
        ts[2] = (tr[1] + tr[2]) + (tr[3] + tr[4])
        send(ts.at[2], tr.at[5], t3s, t3r, at(zl, x, s_h))

    w5_wait()
    picked = lax.broadcasted_iota(jnp.int32, (CH, 128), 1) == (
        lax.broadcasted_iota(jnp.int32, (CH, 128), 0) + CH * x
    )
    picks = jnp.where(picked, 1.0, 0.0).astype(BF16)
    for z in range(NZ):
        block = wall[:, :, :, pl.ds(128 * z, 128)].reshape(C, 128)
        rows = lax.dot_general(picks, block, (((1,), (1,)), ((), ())), preferred_element_type=F32)
        wt[z] = rows.astype(BF16)

    for j in range(CHUNKS):
        grad_gather.arrive(j)
        if j == 0:
            taps_y()

    d1s, d1r = slots.take(1), slots.take(1)
    d2s, d2r = slots.take(2 * NY), slots.take(2 * NY)
    d3s, d3r = slots.take(NS), slots.take(NS)
    d4s_sem, d4r_sem = slots.take(1), slots.take(1)
    own_grad = mg_all[:, pl.ds(x, 1), :, :].reshape(NZ * CH, PART)
    for i in range(4):
        part = lax.dot_general(
            own_grad, vol_all[pl.ds(2 * i, 2)].reshape(C // 4, PART),
            (((1,), (1,)), ((), ())), preferred_element_type=F32,
        )
        part = part.reshape(NZ, 2, CH // 2, C // 4)
        dw[:, :, :, pl.ds(256 * i, 256)] = part
        dwb[:, :, :, pl.ds(256 * i, 256)] = part.astype(BF16)
    send(dwb.at[:, 1 - c], d1b, d1s, d1r, at(zl, x, s_c))
    taps_z()

    rows_own = wt[...].reshape(NZ * CH, C)

    def back(j):
        grad_gather.finish(j)
        multiply(rows_own, mg_all, j, bq)
        back_scatter.start(j)

    back(0)
    recv(d1b, d1r, at(zl, x, s_c))
    summed = d1b[...].astype(F32) + dw[:, pl.ds(c, 1)].reshape(NZ, CH // 2, C)
    d1[...] = summed
    a1b[...] = summed.astype(BF16)
    for t in range(1, NY):
        for h in range(2):
            cols = lanes(128 * (4 * h + rem(y + t, NY)), 128)
            send(a1b.at[:, :, cols], d2.at[t - 1, h], d2s + 2 * t + h, d2r + 2 * t + h, at(zl, x, space_y(t)))
    back(1)
    for h in range(2):
        summed = d1[:, :, lanes(128 * (4 * h + y), 128)]
        for t in range(1, NY):
            recv(d2.at[t - 1, h], d2r + 2 * t + h, at(zl, x, space_y(NY - t)))
            summed = summed + d2[t - 1, h].astype(F32)
        a2[h] = summed
        a2b[h] = summed.astype(BF16)
    z_own = zh * NZ + zl

    def ring(t):
        z = rem(z_own + t, NS)
        return div(z, NZ), rem(z, NZ)

    for t in (8, 7, 9, 6, 10, 5, 11, 4, 12, 3, 13, 2, 14, 1, 15):
        h, z = ring(t)
        send(a2b.at[h, z], d3.at[t - 1], d3s + t, d3r + t, at(z, x, h * 8 + y * 2 + c))
    back(2)
    back(3)
    total = a2[zh, zl]
    for t in range(1, NS):
        h, z = ring(NS - t)
        recv(d3.at[t - 1], d3r + t, at(z, x, h * 8 + y * 2 + c))
        total = total + d3[t - 1].astype(F32)
    d4s[...] = total
    send(d4s, d4r, d4s_sem, d4r_sem, at(zl, x, s_c))

    for z in range(NZ):
        back_scatter.wait(z)

    @pl.loop(0, SLAB // 128)
    def _(j):
        cells = lanes(128 * j, 128)
        vgrad[:, cells] = (up[:, cells].astype(F32) + bb[:, cells].astype(F32)).astype(BF16)

    recv(tr.at[5], t3r, at(zl, x, s_h))
    tgrad[...] = ((ts[2] + tr[5]) * norm)[:, :27]
    recv(d4r, d4r_sem, at(zl, x, s_c))
    even = c == 0
    full = jnp.concatenate(
        [jnp.where(even, d4s[...], d4r[...]), jnp.where(even, d4r[...], d4s[...])], axis=0
    )
    mgrad[...] = jnp.where(even, full[:, :64], full[:, 64:]) * norm

    for cp in pending:
        cp.wait_send()
    pl.when(sends_low)(lambda: m_low().wait_send())
    pl.when(sends_high)(lambda: m_high().wait_send())
    pl.when(has_low)(lambda: g_low().wait_send())
    pl.when(has_high)(lambda: g_high().wait_send())
    grad_gather.drain()

    @pl.when(cross_sends)
    def _():
        for j in range(CHUNKS):
            for z in range(NZ):
                cross_copy(z, j).wait_send()

    assert slots.used <= N_SEMS, slots.used


def body(volume, mixing, kernel_taps, upstream):
    norm = 1.0 / math.sqrt(PLANES * NS * CELLS)
    vmem = pl.BlockSpec(memory_space=pltpu.VMEM)
    scratch = [
        ((CH, SLAB), BF16),
        ((CH, SLAB), BF16),
        ((NZ, NX, CH, PART), BF16),
        ((NZ, NX, CH, PART), BF16),
        ((NZ, NX, CH, C), BF16),
        ((NZ, CH, C), BF16),
        ((NZ, CH, PART), BF16),
        ((NZ, CH, PART), BF16),
        ((CH, 6 * CELLS), BF16),
        ((48, CH, 128), F32),
        ((48, CH, 128), F32),
        ((32, CH, 128), F32),
        ((CH, SLAB), BF16),
        ((CH, 2 * CELLS), BF16),
        ((CH, SLAB), BF16),
        ((CH, SLAB), BF16),
        ((27, CH, 128), F32),
        ((27, CH, 128), F32),
        ((3, CH, 128), F32),
        ((6, CH, 128), F32),
        ((NZ, 2, CH // 2, C), F32),
        ((NZ, 2, CH // 2, C), BF16),
        ((NZ, CH // 2, C), F32),
        ((NZ, CH // 2, C), BF16),
        ((NZ, CH // 2, C), BF16),
        ((3, 2, NZ, CH // 2, 128), BF16),
        ((2, NZ, CH // 2, 128), F32),
        ((2, NZ, CH // 2, 128), BF16),
        ((NS - 1, CH // 2, 128), BF16),
        ((CH // 2, 128), F32),
        ((CH // 2, 128), F32),
    ]
    output, volume_grad, mixing_grad, taps_grad = pl.pallas_call(
        functools.partial(kernel, norm),
        out_shape=(
            jax.ShapeDtypeStruct((CH, SLAB), BF16),
            jax.ShapeDtypeStruct((CH, SLAB), BF16),
            jax.ShapeDtypeStruct((CH, C // NS), F32),
            jax.ShapeDtypeStruct((CH, 27), F32),
        ),
        in_specs=[vmem] * 4,
        out_specs=(vmem,) * 4,
        scratch_shapes=[pltpu.VMEM(*one) for one in scratch] + [pltpu.SemaphoreType.DMA((N_SEMS,)), pltpu.SemaphoreType.REGULAR((2,))],
        compiler_params=pltpu.CompilerParams(collective_id=0, has_side_effects=True),
        name="conv_block",
    )(volume, upstream, mixing, kernel_taps)

    def finish(o_ref, v_ref, m_ref, t_ref, out, vgrad, mgrad, tgrad):
        for i in range(0, CH, 8):
            rows = pl.ds(i, 8)
            out[rows] = (lambda v: v.reshape(8, PLANES, CELLS))(o_ref[rows])
            vgrad[rows] = (lambda v: v.reshape(8, PLANES, CELLS))(v_ref[rows])
        mgrad[...] = m_ref[...]
        tgrad[...] = t_ref[...]

    return pl.pallas_call(
        finish,
        out_shape=(
            jax.ShapeDtypeStruct((CH, PLANES, CELLS), BF16),
            jax.ShapeDtypeStruct((CH, PLANES, CELLS), BF16),
            jax.ShapeDtypeStruct((CH, C // NS), F32),
            jax.ShapeDtypeStruct((CH, 27), F32),
        ),
        in_specs=[vmem] * 4,
        out_specs=(vmem,) * 4,
        name="by_planes",
    )(output, volume_grad, mixing_grad, taps_grad)


def solution(mesh):
    channel_slab = P("filter", "space", None)
    return jax.shard_map(
        body,
        mesh=mesh,
        in_specs=(channel_slab, P("filter", None), P("filter", None), channel_slab),
        out_specs=(channel_slab, channel_slab, P("filter", "space"), P("filter", None)),
        check_vma=False,
    )
```

```python
import functools
import math

import jax
import jax.numpy as jnp
from jax import lax
from jax.experimental import pallas as pl
from jax.experimental.pallas import tpu as pltpu
from jax.sharding import PartitionSpec as P

F32 = jnp.float32
BF16 = jnp.bfloat16
MESH = pl.DeviceIdType.MESH

NZ, NX, NY = 8, 4, 4
NF, NS = 32, 16
CH = 32
PLANES, CELLS, WW = 4, 1024, 64
SLAB = PLANES * CELLS
PART = SLAB // NZ
C = NF * CH
CHUNKS = 4
WIDTH = PART // CHUNKS
ORDER = (4, 3, 5, 2, 6, 1, 7)


class Slots:
    def __init__(self):
        self.used = 0

    def take(self, n):
        first = self.used
        self.used += n
        return first


N_SEMS = 480


def kernel(
    norm, vol_planes, up_planes, mix, taps, out, vgrad, mgrad, tgrad,
    vol, up, vol_all, mg_all, wall, wt, mq, bq, mb, m32, sg32, sp32, sgb, sgh, mgb, bb, tb, tg, ts, tr,
    dw, dwb, d1, d1b, a1b, d2, a2, a2b, d3, d4s, d4r, sems, token,
):
    f = lax.axis_index("filter")
    s = lax.axis_index("space")

    def div(a, b):
        return lax.div(a, jnp.int32(b))

    def rem(a, b):
        return lax.rem(a, jnp.int32(b))

    zl, x = div(f, NX), rem(f, NX)
    zh, c = div(s, 8), rem(s, 2)
    y = div(rem(s, 8), 2)
    s_c = s + 1 - 2 * c
    s_n = zh * 8 + rem(rem(s, 8) + 7 + 2 * c, 8)
    s_h = rem(s + 8, NS)

    def at(zl_, x_, s_):
        return {"filter": zl_ * NX + x_, "space": s_}

    def lanes(start, size):
        return pl.ds(pl.multiple_of(start, 128), size)

    def chunk(j):
        return pl.ds(WIDTH * j, WIDTH)

    slots = Slots()
    pending = []

    def copy_to(src, dst, ss, rs, where):
        return pltpu.make_async_remote_copy(
            src_ref=src, dst_ref=dst, send_sem=sems.at[ss], recv_sem=sems.at[rs],
            device_id=where, device_id_type=MESH,
        )

    def send(src, dst, ss, rs, where):
        cp = copy_to(src, dst, ss, rs, where)
        cp.start()
        pending.append(cp)

    def recv(dst, rs, where):
        copy_to(dst, dst, rs, rs, where).wait_recv()

    barrier = pltpu.get_barrier_semaphore()
    peers = [at(rem(zl + t, NZ), x, s) for t in range(1, NZ)]
    peers += [at(zl, rem(x + t, NX), s) for t in range(1, NX)]
    peers += [at(zl, x, s_c), at(zl, x, s_n)]
    peers += [at(zl, x, zh * 8 + rem(y + t, NY) * 2 + c) for t in range(1, NY)]
    for peer in peers:
        pl.semaphore_signal(barrier, inc=1, device_id=peer, device_id_type=MESH)

    edge = ((zl == 0) & (zh == 0)) | ((zl == NZ - 1) & (zh == 1))
    partner = at(NZ - 1 - zl, x, s_h)

    @pl.when(edge)
    def _():
        pl.semaphore_signal(barrier, inc=1, device_id=partner, device_id_type=MESH)

    for i in range(0, CH, 8):
        rows = pl.ds(i, 8)
        vol[rows] = (lambda v: v.reshape(8, SLAB))(vol_planes[rows])
        up[rows] = (lambda v: v.reshape(8, SLAB))(up_planes[rows])

    def tell(i, where):
        pl.semaphore_signal(token.at[i], inc=1, device_id=where, device_id_type=MESH)

    @pl.when(edge)
    def _():
        pl.semaphore_wait(barrier, len(peers) + 1)
        tell(0, partner)

    @pl.when(jnp.logical_not(edge))
    def _():
        pl.semaphore_wait(barrier, len(peers))

    def other_half_to_column():
        @pl.when(edge)
        def _():
            pl.semaphore_wait(token.at[0], 1)
            for t in range(1, NZ):
                tell(0, at(rem(zl + t, NZ), x, s))

    def other_half_known():
        pl.when(jnp.logical_not(edge))(lambda: pl.semaphore_wait(token.at[0], 1))
        pl.when(s == 0)(lambda: tell(1, at(zl, x, 7)))
        pl.when(s == NS - 1)(lambda: tell(1, at(zl, x, 8)))
        pl.when((s == 7) | (s == 8))(lambda: pl.semaphore_wait(token.at[1], 1))

    class Gather:
        def __init__(self, src, dst):
            self.src, self.dst = src, dst
            self.zs, self.zr = slots.take(NZ * CHUNKS), slots.take(NZ * CHUNKS)
            self.xs, self.xr = slots.take(NX * CHUNKS), slots.take(NX * CHUNKS)

        def start(self):
            for j in range(CHUNKS):
                for t in ORDER:
                    zt = rem(zl + t, NZ)
                    send(self.src.at[:, lanes(PART * zt + WIDTH * j, WIDTH)], self.dst.at[zl, x, :, chunk(j)],
                         self.zs + NZ * j + t, self.zr + NZ * j + t, at(zt, x, s))
            self.dst[zl, x] = self.src[:, lanes(PART * zl, PART)]

        def take(self, j):
            for t in ORDER:
                zf = rem(zl + NZ - t, NZ)
                recv(self.dst.at[zf, x, :, chunk(j)], self.zr + NZ * j + t, at(zf, x, s))

        def arrive(self, j):
            self.take(j)
            part = self.dst.at[:, x, :, chunk(j)]
            for t in (2, 1, 3):
                send(part, part, self.xs + NX * j + t, self.xr + NX * j + t, at(zl, rem(x + t, NX), s))

        def finish(self, j):
            for t in (1, 3, 2):
                xf = rem(x + NX - t, NX)
                recv(self.dst.at[:, xf, :, chunk(j)], self.xr + NX * j + t, at(zl, xf, s))

    class PlaneGather(Gather):
        def piece(self, q, j):
            return copy_to(self.src.at[:, pl.ds(PART * q + WIDTH * j, WIDTH)], self.dst.at[zl, x, :, chunk(j)],
                           self.zs + NZ * j + q, self.zr + NZ * j + zl, at(q, x, s))

        def start(self, parts):
            for j in range(CHUNKS):
                for q in parts:
                    pl.when(zl != q)(lambda: self.piece(q, j).start())

        def own(self):
            self.dst[zl, x] = self.src[:, lanes(PART * zl, PART)]

        def take(self, j):
            for z in range(NZ):
                @pl.when(zl != z)
                def _():
                    recv(self.dst.at[z, x, :, chunk(j)], self.zr + NZ * j + z, at(z, x, s))

        def drain(self):
            for q in range(NZ):
                @pl.when(zl != q)
                def _():
                    for j in range(CHUNKS):
                        self.piece(q, j).wait_send()

    class Scatter:
        def __init__(self, src, dst, offset):
            self.src, self.dst, self.offset = src, dst, offset
            self.ss, self.sr = slots.take(NZ * CHUNKS), slots.take(NZ * CHUNKS)

        def place(self, z, j):
            return self.dst.at[:, lanes(self.offset + PART * z + WIDTH * j, WIDTH)]

        def start(self, j):
            for t in ORDER:
                zt = rem(zl + t, NZ)
                send(self.src.at[zt, :, chunk(j)], self.place(zl, j),
                     self.ss + NZ * j + t, self.sr + NZ * j + zl, at(zt, x, s))
            self.dst[:, lanes(self.offset + PART * zl + WIDTH * j, WIDTH)] = self.src[zl, :, chunk(j)]

        def wait(self, z):
            @pl.when(zl != z)
            def _():
                for j in range(CHUNKS):
                    recv(self.place(z, j), self.sr + NZ * j + z, at(z, x, s))

    def multiply(weights, data, j, dst):
        product = jnp.dot(weights, data[:, :, :, chunk(j)].reshape(C, WIDTH), preferred_element_type=F32)
        dst[:, :, chunk(j)] = product.astype(BF16).reshape(NZ, CH, WIDTH)

    k = c * 4 + y
    own_cols = lanes(128 * k, 128)
    side = lanes(512 * c, 512)
    other = lanes(512 * (1 - c), 512)
    w1s, w1r = slots.take(NZ), slots.take(NZ)
    w2s, w2r = slots.take(NY), slots.take(NY)
    w3s, w3r = slots.take(1), slots.take(1)
    w4s, w4r = slots.take(NX), slots.take(NX)
    w5s, w5r = slots.take(NX), slots.take(NX)

    def space_y(t):
        return zh * 8 + rem(y + t, NY) * 2 + c

    def w1_start():
        for t in ORDER:
            send(mix.at[:, own_cols], wall.at[zl, x, :, own_cols], w1s + t, w1r + t, at(rem(zl + t, NZ), x, s))
        wall[zl, x, :, own_cols] = mix[:, own_cols]

    def w2_start():
        for t in ORDER:
            zf = rem(zl + NZ - t, NZ)
            recv(wall.at[zf, x, :, own_cols], w1r + t, at(zf, x, s))
        part = wall.at[:, x, :, own_cols]
        for t in range(1, NY):
            send(part, part, w2s + t, w2r + t, at(zl, x, space_y(t)))

    def w3_start():
        for t in range(1, NY):
            cols = lanes(128 * (c * 4 + rem(y + NY - t, NY)), 128)
            recv(wall.at[:, x, :, cols], w2r + t, at(zl, x, space_y(NY - t)))
        part = wall.at[:, x, :, side]
        send(part, part, w3s, w3r, at(zl, x, s_c))

    def w3_wait():
        recv(wall.at[:, x, :, other], w3r, at(zl, x, s_c))

    def w4_start():
        part = wall.at[:, x, :, side]
        for t in range(1, NX):
            send(part, part, w4s + t, w4r + t, at(zl, rem(x + t, NX), s))

    def w5_start():
        for t in range(1, NX):
            xf = rem(x + NX - t, NX)
            part = wall.at[:, xf, :, side]
            recv(part, w4r + t, at(zl, xf, s))
            send(part, part, w5s + t, w5r + t, at(zl, x, s_c))

    def w5_wait():
        for t in range(1, NX):
            xf = rem(x + NX - t, NX)
            recv(wall.at[:, xf, :, other], w5r + t, at(zl, x, s_c))

    lane = lax.broadcasted_iota(jnp.int32, (8, 8, 128), 2)
    first_col = lax.rem(lane, WW) == 0
    last_col = lax.rem(lane, WW) == WW - 1
    first_row = lane < WW
    zero = jnp.zeros((8, 8, 128), F32)

    def columns(v):
        before = jnp.where(first_col, zero, pltpu.roll(v, 1, 2))
        after = jnp.where(last_col, zero, pltpu.roll(v, 127, 2))
        return before, v, after

    def rows_down(v):
        swapped = pltpu.roll(v, WW, 2)
        above = jnp.concatenate([zero[:1], swapped[:-1]], axis=0)
        return jnp.where(first_row, above, swapped)

    def rows_up(v):
        swapped = pltpu.roll(v, WW, 2)
        below = jnp.concatenate([swapped[1:], zero[:1]], axis=0)
        return jnp.where(first_row, swapped, below)

    def conv(src, d, flip):
        @pl.loop(0, CH // 8)
        def _(g):
            rows = pl.ds(pl.multiple_of(8 * g, 8), 8)
            sums = [None] * 3
            for a in range(3):
                shifted = columns(src[pl.ds(8 * (d + a), 8), rows, :])
                for b in range(3):
                    for e in range(3):
                        tap = 9 * a + 3 * b + e
                        tap = 26 - tap if flip else tap
                        term = tb[tap, rows, :][None] * shifted[e]
                        sums[b] = term if sums[b] is None else sums[b] + term
            sp32[pl.ds(8 * d, 8), rows, :] = rows_down(sums[0]) + sums[1] + rows_up(sums[2])

    def widen(src, start, dst, chunk):
        for j in range(8):
            dst[chunk + j] = src[:, pl.ds(start + 128 * j, 128)].astype(F32)

    def pointwise(d):
        @pl.loop(0, 8)
        def _(j):
            at_chunk = 8 * d + j
            cells = lanes(128 * at_chunk, 128)
            spatial = sp32[at_chunk]
            sig = lax.logistic(spatial)
            grad = up[:, cells].astype(F32) * (sig * (1.0 + spatial * (1.0 - sig)))
            grad = grad.astype(BF16)
            sgb[:, cells] = grad
            sg32[8 + at_chunk] = grad.astype(F32)
            out[:, cells] = (vol[:, cells].astype(F32) + spatial * sig).astype(BF16)

    def forward_planes(first, step, count):
        @pl.loop(0, count)
        def _(i):
            d = first + step * i
            conv(m32, d, False)
            pointwise(d)

    def backward_planes(first, step):
        @pl.loop(0, 2)
        def _(i):
            d = first + step * i
            conv(sg32, d, True)

            @pl.loop(0, 8)
            def _(j):
                mgb[:, lanes(128 * (8 * d + j), 128)] = sp32[8 * d + j].astype(BF16)

    def tap_sums():
        @pl.loop(0, CH // 8)
        def _(g):
            rows = pl.ds(pl.multiple_of(8 * g, 8), 8)
            for tap in range(27):
                tg[tap, rows, :] = zero[0]

            @pl.loop(0, PLANES)
            def _(d):
                grad = sg32[pl.ds(8 * d + 8, 8), rows, :]
                grads = (rows_up(grad), grad, rows_down(grad))
                for a in range(3):
                    shifted = columns(m32[pl.ds(8 * (d + a), 8), rows, :])
                    for b in range(3):
                        for e in range(3):
                            tap = 9 * a + 3 * b + e
                            tg[tap, rows, :] = tg[tap, rows, :] + jnp.sum(grads[b] * shifted[e], axis=0)

        tap_lane = lax.broadcasted_iota(jnp.int32, (CH, 128), 1)
        total = jnp.zeros((CH, 128), F32)
        for tap in range(27):
            total = jnp.where(tap_lane == tap, jnp.sum(tg[tap], axis=1, keepdims=True), total)
        ts[0] = total

    halo_s = [slots.take(2), slots.take(2)]
    halo_r = [slots.take(2), slots.take(2)]
    has_low, has_high = s > 0, s < NS - 1
    sends_low, sends_high = (s > 0) & (s != 8), (s < NS - 1) & (s != 7)

    def halo_low(i, src, dst):
        return copy_to(src, dst, halo_s[i], halo_r[i], at(zl, x, s - 1))

    def halo_high(i, src, dst):
        return copy_to(src, dst, halo_s[i] + 1, halo_r[i] + 1, at(zl, x, s + 1))

    def m_low():
        return halo_low(0, mb.at[:, pl.ds(CELLS, CELLS)], mb.at[:, pl.ds(5 * CELLS, CELLS)])

    def m_high():
        return halo_high(0, mb.at[:, pl.ds(4 * CELLS, CELLS)], mb.at[:, pl.ds(0, CELLS)])

    def g_low():
        return halo_low(1, sgb.at[:, pl.ds(0, CELLS)], sgh.at[:, pl.ds(CELLS, CELLS)])

    def g_high():
        return halo_high(1, sgb.at[:, pl.ds(3 * CELLS, CELLS)], sgh.at[:, pl.ds(0, CELLS)])

    cross_s, cross_r = slots.take(NZ * CHUNKS), slots.take(2 * CHUNKS)
    cross_part = zl - 6 * (8 - s)
    cross_sends = ((s == 7) & (zl >= 6)) | ((s == 8) & (zl <= 1))

    def cross_copy(z, j):
        place = mb.at[:, lanes(5 * CELLS * (s - 7) + PART * cross_part + WIDTH * j, WIDTH)]
        return copy_to(mq.at[z, :, chunk(j)], place, cross_s + NZ * j + z,
                       cross_r + CHUNKS * cross_part + j, at(z, x, 15 - s))

    def cross_start(j):
        @pl.when(cross_sends)
        def _():
            for z in range(NZ):
                cross_copy(z, j).start()

    def cross_arrive(start, first_z):
        for part in range(2):
            for j in range(CHUNKS):
                recv(mb.at[:, pl.ds(start + PART * part + WIDTH * j, WIDTH)],
                     cross_r + CHUNKS * part + j, at(first_z + part, x, 15 - s))

    def mixed_halo_arrive():
        @pl.when((s > 0) & (s != 8))
        def _():
            recv(mb.at[:, pl.ds(0, CELLS)], halo_r[0] + 1, at(zl, x, s - 1))

        pl.when(s == 8)(lambda: cross_arrive(0, 6))

        @pl.when((s < NS - 1) & (s != 7))
        def _():
            recv(mb.at[:, pl.ds(5 * CELLS, CELLS)], halo_r[0], at(zl, x, s + 1))

        pl.when(s == 7)(lambda: cross_arrive(5 * CELLS, 0))
        for edge, start, row in ((s == 0, 0, 0), (s == NS - 1, 5 * CELLS, 40)):
            @pl.when(edge)
            def _():
                for j in range(8):
                    m32[row + j] = jnp.zeros((CH, 128), F32)

            @pl.when(jnp.logical_not(edge))
            def _():
                widen(mb, start, m32, row)

    def halo_arrive(i, low_ref, low_at, high_ref, high_at, dst):
        @pl.when(has_low)
        def _():
            recv(low_ref.at[:, pl.ds(low_at, CELLS)], halo_r[i] + 1, at(zl, x, s - 1))
            widen(low_ref, low_at, dst, 0)

        @pl.when(s == 0)
        def _():
            for j in range(8):
                dst[j] = jnp.zeros((CH, 128), F32)

        @pl.when(has_high)
        def _():
            recv(high_ref.at[:, pl.ds(high_at, CELLS)], halo_r[i], at(zl, x, s + 1))
            widen(high_ref, high_at, dst, 40)

        @pl.when(s == NS - 1)
        def _():
            for j in range(8):
                dst[40 + j] = jnp.zeros((CH, 128), F32)

    volume_gather = Gather(vol, vol_all)
    grad_gather = PlaneGather(mgb, mg_all)
    mixed_scatter = Scatter(mq, mb, CELLS)
    back_scatter = Scatter(bq, bb, 0)

    w1_start()
    volume_gather.start()
    for tap in range(27):
        tb[tap] = jnp.broadcast_to(taps[:, tap : tap + 1], (CH, 128))
    w2_start()
    other_half_to_column()
    for j in range(CHUNKS):
        volume_gather.arrive(j)
        if j == 1:
            w3_start()
    w3_wait()
    columns_own = wall[:, pl.ds(x, 1), :, :].reshape(NZ * CH, C)
    for j in range(CHUNKS):
        volume_gather.finish(j)
        multiply(columns_own, vol_all, j, mq)
        mixed_scatter.start(j)
        if j == 0:
            other_half_known()
        cross_start(j)
    w4_start()
    for z in (0, 1):
        mixed_scatter.wait(z)
    pl.when(sends_low)(lambda: m_low().start())
    for z in (6, 7):
        mixed_scatter.wait(z)
    pl.when(sends_high)(lambda: m_high().start())
    for z in (2, 3, 4, 5):
        mixed_scatter.wait(z)

    for d in range(PLANES):
        widen(mb, CELLS * (d + 1), m32, 8 * (d + 1))
    forward_planes(1, 1, 1)
    mixed_halo_arrive()
    forward_planes(0, 3, 2)
    pl.when(has_low)(lambda: g_low().start())
    pl.when(has_high)(lambda: g_high().start())
    w5_start()

    forward_planes(2, 1, 1)
    backward_planes(1, 1)
    grad_gather.start((3, 4, 2, 5))
    tap_sums()
    halo_arrive(1, sgh, 0, sgh, CELLS, sg32)
    backward_planes(0, 3)
    grad_gather.start((0, 7, 1, 6))
    grad_gather.own()

    t1s, t1r = slots.take(1), slots.take(1)
    t2s, t2r = slots.take(NY), slots.take(NY)
    t3s, t3r = slots.take(1), slots.take(1)
    send(ts.at[0], tr.at[0], t1s, t1r, at(zl, x, s_c))

    def taps_y():
        recv(tr.at[0], t1r, at(zl, x, s_c))
        ts[1] = ts[0] + tr[0]
        for t in range(1, NY):
            send(ts.at[1], tr.at[1 + y], t2s + t, t2r + t, at(zl, x, space_y(t)))
        tr[1 + y] = ts[1]

    def taps_z():
        for t in range(1, NY):
            recv(tr.at[1 + rem(y + NY - t, NY)], t2r + t, at(zl, x, space_y(NY - t)))
        ts[2] = (tr[1] + tr[2]) + (tr[3] + tr[4])
        send(ts.at[2], tr.at[5], t3s, t3r, at(zl, x, s_h))

    w5_wait()
    picked = lax.broadcasted_iota(jnp.int32, (CH, 128), 1) == (
        lax.broadcasted_iota(jnp.int32, (CH, 128), 0) + CH * x
    )
    picks = jnp.where(picked, 1.0, 0.0).astype(BF16)
    for z in range(NZ):
        block = wall[:, :, :, pl.ds(128 * z, 128)].reshape(C, 128)
        rows = lax.dot_general(picks, block, (((1,), (1,)), ((), ())), preferred_element_type=F32)
        wt[z] = rows.astype(BF16)

    for j in range(CHUNKS):
        grad_gather.arrive(j)
        if j == 0:
            taps_y()

    d1s, d1r = slots.take(1), slots.take(1)
    d2s, d2r = slots.take(2 * NY), slots.take(2 * NY)
    d3s, d3r = slots.take(NS), slots.take(NS)
    d4s_sem, d4r_sem = slots.take(1), slots.take(1)
    own_grad = mg_all[:, pl.ds(x, 1), :, :].reshape(NZ * CH, PART)
    for i in range(4):
        part = lax.dot_general(
            own_grad, vol_all[pl.ds(2 * i, 2)].reshape(C // 4, PART),
            (((1,), (1,)), ((), ())), preferred_element_type=F32,
        )
        part = part.reshape(NZ, 2, CH // 2, C // 4)
        dw[:, :, :, pl.ds(256 * i, 256)] = part
        dwb[:, :, :, pl.ds(256 * i, 256)] = part.astype(BF16)
    send(dwb.at[:, 1 - c], d1b, d1s, d1r, at(zl, x, s_c))
    taps_z()

    rows_own = wt[...].reshape(NZ * CH, C)

    def back(j):
        grad_gather.finish(j)
        multiply(rows_own, mg_all, j, bq)
        back_scatter.start(j)

    back(0)
    recv(d1b, d1r, at(zl, x, s_c))
    summed = d1b[...].astype(F32) + dw[:, pl.ds(c, 1)].reshape(NZ, CH // 2, C)
    d1[...] = summed
    a1b[...] = summed.astype(BF16)
    for t in range(1, NY):
        for h in range(2):
            cols = lanes(128 * (4 * h + rem(y + t, NY)), 128)
            send(a1b.at[:, :, cols], d2.at[t - 1, h], d2s + 2 * t + h, d2r + 2 * t + h, at(zl, x, space_y(t)))
    back(1)
    for h in range(2):
        summed = d1[:, :, lanes(128 * (4 * h + y), 128)]
        for t in range(1, NY):
            recv(d2.at[t - 1, h], d2r + 2 * t + h, at(zl, x, space_y(NY - t)))
            summed = summed + d2[t - 1, h].astype(F32)
        a2[h] = summed
        a2b[h] = summed.astype(BF16)
    z_own = zh * NZ + zl

    def ring(t):
        z = rem(z_own + t, NS)
        return div(z, NZ), rem(z, NZ)

    for t in (8, 7, 9, 6, 10, 5, 11, 4, 12, 3, 13, 2, 14, 1, 15):
        h, z = ring(t)
        send(a2b.at[h, z], d3.at[t - 1], d3s + t, d3r + t, at(z, x, h * 8 + y * 2 + c))
    back(2)
    back(3)
    total = a2[zh, zl]
    for t in range(1, NS):
        h, z = ring(NS - t)
        recv(d3.at[t - 1], d3r + t, at(z, x, h * 8 + y * 2 + c))
        total = total + d3[t - 1].astype(F32)
    d4s[...] = total
    send(d4s, d4r, d4s_sem, d4r_sem, at(zl, x, s_c))

    for z in range(NZ):
        back_scatter.wait(z)

    @pl.loop(0, SLAB // 128)
    def _(j):
        cells = lanes(128 * j, 128)
        vgrad[:, cells] = (up[:, cells].astype(F32) + bb[:, cells].astype(F32)).astype(BF16)

    recv(tr.at[5], t3r, at(zl, x, s_h))
    tgrad[...] = ((ts[2] + tr[5]) * norm)[:, :27]
    recv(d4r, d4r_sem, at(zl, x, s_c))
    even = c == 0
    full = jnp.concatenate(
        [jnp.where(even, d4s[...], d4r[...]), jnp.where(even, d4r[...], d4s[...])], axis=0
    )
    mgrad[...] = jnp.where(even, full[:, :64], full[:, 64:]) * norm

    for cp in pending:
        cp.wait_send()
    pl.when(sends_low)(lambda: m_low().wait_send())
    pl.when(sends_high)(lambda: m_high().wait_send())
    pl.when(has_low)(lambda: g_low().wait_send())
    pl.when(has_high)(lambda: g_high().wait_send())
    grad_gather.drain()

    @pl.when(cross_sends)
    def _():
        for j in range(CHUNKS):
            for z in range(NZ):
                cross_copy(z, j).wait_send()

    assert slots.used <= N_SEMS, slots.used


def body(volume, mixing, kernel_taps, upstream):
    norm = 1.0 / math.sqrt(PLANES * NS * CELLS)
    vmem = pl.BlockSpec(memory_space=pltpu.VMEM)
    scratch = [
        ((CH, SLAB), BF16),
        ((CH, SLAB), BF16),
        ((NZ, NX, CH, PART), BF16),
        ((NZ, NX, CH, PART), BF16),
        ((NZ, NX, CH, C), BF16),
        ((NZ, CH, C), BF16),
        ((NZ, CH, PART), BF16),
        ((NZ, CH, PART), BF16),
        ((CH, 6 * CELLS), BF16),
        ((48, CH, 128), F32),
        ((48, CH, 128), F32),
        ((32, CH, 128), F32),
        ((CH, SLAB), BF16),
        ((CH, 2 * CELLS), BF16),
        ((CH, SLAB), BF16),
        ((CH, SLAB), BF16),
        ((27, CH, 128), F32),
        ((27, CH, 128), F32),
        ((3, CH, 128), F32),
        ((6, CH, 128), F32),
        ((NZ, 2, CH // 2, C), F32),
        ((NZ, 2, CH // 2, C), BF16),
        ((NZ, CH // 2, C), F32),
        ((NZ, CH // 2, C), BF16),
        ((NZ, CH // 2, C), BF16),
        ((3, 2, NZ, CH // 2, 128), BF16),
        ((2, NZ, CH // 2, 128), F32),
        ((2, NZ, CH // 2, 128), BF16),
        ((NS - 1, CH // 2, 128), BF16),
        ((CH // 2, 128), F32),
        ((CH // 2, 128), F32),
    ]
    output, volume_grad, mixing_grad, taps_grad = pl.pallas_call(
        functools.partial(kernel, norm),
        out_shape=(
            jax.ShapeDtypeStruct((CH, SLAB), BF16),
            jax.ShapeDtypeStruct((CH, SLAB), BF16),
            jax.ShapeDtypeStruct((CH, C // NS), F32),
            jax.ShapeDtypeStruct((CH, 27), F32),
        ),
        in_specs=[vmem] * 4,
        out_specs=(vmem,) * 4,
        scratch_shapes=[pltpu.VMEM(*one) for one in scratch] + [pltpu.SemaphoreType.DMA((N_SEMS,)), pltpu.SemaphoreType.REGULAR((2,))],
        compiler_params=pltpu.CompilerParams(collective_id=0, has_side_effects=True),
        name="conv_block",
    )(volume, upstream, mixing, kernel_taps)

    def finish(o_ref, v_ref, m_ref, t_ref, out, vgrad, mgrad, tgrad):
        for i in range(0, CH, 8):
            rows = pl.ds(i, 8)
            out[rows] = (lambda v: v.reshape(8, PLANES, CELLS))(o_ref[rows])
            vgrad[rows] = (lambda v: v.reshape(8, PLANES, CELLS))(v_ref[rows])
        mgrad[...] = m_ref[...]
        tgrad[...] = t_ref[...]

    return pl.pallas_call(
        finish,
        out_shape=(
            jax.ShapeDtypeStruct((CH, PLANES, CELLS), BF16),
            jax.ShapeDtypeStruct((CH, PLANES, CELLS), BF16),
            jax.ShapeDtypeStruct((CH, C // NS), F32),
            jax.ShapeDtypeStruct((CH, 27), F32),
        ),
        in_specs=[vmem] * 4,
        out_specs=(vmem,) * 4,
        name="by_planes",
    )(output, volume_grad, mixing_grad, taps_grad)


def solution(mesh):
    channel_slab = P("filter", "space", None)
    return jax.shard_map(
        body,
        mesh=mesh,
        in_specs=(channel_slab, P("filter", None), P("filter", None), channel_slab),
        out_specs=(channel_slab, channel_slab, P("filter", "space"), P("filter", None)),
        check_vma=False,
    )
```

```python
import functools
import math

import jax
import jax.numpy as jnp
from jax import lax
from jax.experimental import pallas as pl
from jax.experimental.pallas import tpu as pltpu
from jax.sharding import PartitionSpec as P

F32 = jnp.float32
BF16 = jnp.bfloat16
MESH = pl.DeviceIdType.MESH

NZ, NX, NY = 8, 4, 4
NF, NS = 32, 16
CH = 32
PLANES, CELLS, WW = 4, 1024, 64
SLAB = PLANES * CELLS
PART = SLAB // NZ
C = NF * CH
CHUNKS = 4
WIDTH = PART // CHUNKS
ORDER = (4, 3, 5, 2, 6, 1, 7)


class Slots:
    def __init__(self):
        self.used = 0

    def take(self, n):
        first = self.used
        self.used += n
        return first


N_SEMS = 480


def kernel(
    norm, vol_planes, up_planes, mix, taps, out, vgrad, mgrad, tgrad,
    vol, up, vol_all, mg_all, wall, wt, mq, bq, mb, m32, sg32, sp32, sgb, sgh, mgb, bb, tb, tg, ts, tr,
    dw, dwb, d1, d1b, a1b, d2, a2, a2b, d3, d4s, d4r, sems, token,
):
    f = lax.axis_index("filter")
    s = lax.axis_index("space")

    def div(a, b):
        return lax.div(a, jnp.int32(b))

    def rem(a, b):
        return lax.rem(a, jnp.int32(b))

    zl, x = div(f, NX), rem(f, NX)
    zh, c = div(s, 8), rem(s, 2)
    y = div(rem(s, 8), 2)
    s_c = s + 1 - 2 * c
    s_n = zh * 8 + rem(rem(s, 8) + 7 + 2 * c, 8)
    s_h = rem(s + 8, NS)

    def at(zl_, x_, s_):
        return {"filter": zl_ * NX + x_, "space": s_}

    def lanes(start, size):
        return pl.ds(pl.multiple_of(start, 128), size)

    def chunk(j):
        return pl.ds(WIDTH * j, WIDTH)

    slots = Slots()
    pending = []

    def copy_to(src, dst, ss, rs, where):
        return pltpu.make_async_remote_copy(
            src_ref=src, dst_ref=dst, send_sem=sems.at[ss], recv_sem=sems.at[rs],
            device_id=where, device_id_type=MESH,
        )

    def send(src, dst, ss, rs, where):
        cp = copy_to(src, dst, ss, rs, where)
        cp.start()
        pending.append(cp)

    def recv(dst, rs, where):
        copy_to(dst, dst, rs, rs, where).wait_recv()

    barrier = pltpu.get_barrier_semaphore()
    peers = [at(rem(zl + t, NZ), x, s) for t in range(1, NZ)]
    peers += [at(zl, rem(x + t, NX), s) for t in range(1, NX)]
    peers += [at(zl, x, s_c), at(zl, x, s_n)]
    peers += [at(zl, x, zh * 8 + rem(y + t, NY) * 2 + c) for t in range(1, NY)]
    for peer in peers:
        pl.semaphore_signal(barrier, inc=1, device_id=peer, device_id_type=MESH)

    edge = ((zl == 0) & (zh == 0)) | ((zl == NZ - 1) & (zh == 1))
    partner = at(NZ - 1 - zl, x, s_h)

    @pl.when(edge)
    def _():
        pl.semaphore_signal(barrier, inc=1, device_id=partner, device_id_type=MESH)

    for i in range(0, CH, 8):
        rows = pl.ds(i, 8)
        vol[rows] = (lambda v: v.reshape(8, SLAB))(vol_planes[rows])
        up[rows] = (lambda v: v.reshape(8, SLAB))(up_planes[rows])

    def tell(i, where):
        pl.semaphore_signal(token.at[i], inc=1, device_id=where, device_id_type=MESH)

    @pl.when(edge)
    def _():
        pl.semaphore_wait(barrier, len(peers) + 1)
        tell(0, partner)

    @pl.when(jnp.logical_not(edge))
    def _():
        pl.semaphore_wait(barrier, len(peers))

    def other_half_to_column():
        @pl.when(edge)
        def _():
            pl.semaphore_wait(token.at[0], 1)
            for t in range(1, NZ):
                tell(0, at(rem(zl + t, NZ), x, s))

    def other_half_known():
        pl.when(jnp.logical_not(edge))(lambda: pl.semaphore_wait(token.at[0], 1))
        pl.when(s == 0)(lambda: tell(1, at(zl, x, 7)))
        pl.when(s == NS - 1)(lambda: tell(1, at(zl, x, 8)))
        pl.when((s == 7) | (s == 8))(lambda: pl.semaphore_wait(token.at[1], 1))

    class Gather:
        def __init__(self, src, dst):
            self.src, self.dst = src, dst
            self.zs, self.zr = slots.take(NZ * CHUNKS), slots.take(NZ * CHUNKS)
            self.xs, self.xr = slots.take(NX * CHUNKS), slots.take(NX * CHUNKS)

        def start(self):
            for j in range(CHUNKS):
                for t in ORDER:
                    zt = rem(zl + t, NZ)
                    send(self.src.at[:, lanes(PART * zt + WIDTH * j, WIDTH)], self.dst.at[zl, x, :, chunk(j)],
                         self.zs + NZ * j + t, self.zr + NZ * j + t, at(zt, x, s))
            self.dst[zl, x] = self.src[:, lanes(PART * zl, PART)]

        def take(self, j):
            for t in ORDER:
                zf = rem(zl + NZ - t, NZ)
                recv(self.dst.at[zf, x, :, chunk(j)], self.zr + NZ * j + t, at(zf, x, s))

        def arrive(self, j):
            self.take(j)
            part = self.dst.at[:, x, :, chunk(j)]
            for t in (2, 1, 3):
                send(part, part, self.xs + NX * j + t, self.xr + NX * j + t, at(zl, rem(x + t, NX), s))

        def finish(self, j):
            for t in (1, 3, 2):
                xf = rem(x + NX - t, NX)
                recv(self.dst.at[:, xf, :, chunk(j)], self.xr + NX * j + t, at(zl, xf, s))

    class PlaneGather(Gather):
        def piece(self, q, j):
            return copy_to(self.src.at[:, pl.ds(PART * q + WIDTH * j, WIDTH)], self.dst.at[zl, x, :, chunk(j)],
                           self.zs + NZ * j + q, self.zr + NZ * j + zl, at(q, x, s))

        def start(self, parts):
            for j in range(CHUNKS):
                for q in parts:
                    pl.when(zl != q)(lambda: self.piece(q, j).start())

        def own(self):
            self.dst[zl, x] = self.src[:, lanes(PART * zl, PART)]

        def take(self, j):
            for z in range(NZ):
                @pl.when(zl != z)
                def _():
                    recv(self.dst.at[z, x, :, chunk(j)], self.zr + NZ * j + z, at(z, x, s))

        def drain(self):
            for q in range(NZ):
                @pl.when(zl != q)
                def _():
                    for j in range(CHUNKS):
                        self.piece(q, j).wait_send()

    class Scatter:
        def __init__(self, src, dst, offset):
            self.src, self.dst, self.offset = src, dst, offset
            self.ss, self.sr = slots.take(NZ * CHUNKS), slots.take(NZ * CHUNKS)

        def place(self, z, j):
            return self.dst.at[:, lanes(self.offset + PART * z + WIDTH * j, WIDTH)]

        def start(self, j):
            for t in ORDER:
                zt = rem(zl + t, NZ)
                send(self.src.at[zt, :, chunk(j)], self.place(zl, j),
                     self.ss + NZ * j + t, self.sr + NZ * j + zl, at(zt, x, s))
            self.dst[:, lanes(self.offset + PART * zl + WIDTH * j, WIDTH)] = self.src[zl, :, chunk(j)]

        def wait(self, z):
            @pl.when(zl != z)
            def _():
                for j in range(CHUNKS):
                    recv(self.place(z, j), self.sr + NZ * j + z, at(z, x, s))

    def multiply(weights, data, j, dst):
        product = jnp.dot(weights, data[:, :, :, chunk(j)].reshape(C, WIDTH), preferred_element_type=F32)
        dst[:, :, chunk(j)] = product.astype(BF16).reshape(NZ, CH, WIDTH)

    k = c * 4 + y
    own_cols = lanes(128 * k, 128)
    side = lanes(512 * c, 512)
    other = lanes(512 * (1 - c), 512)
    w1s, w1r = slots.take(NZ), slots.take(NZ)
    w2s, w2r = slots.take(NY), slots.take(NY)
    w3s, w3r = slots.take(1), slots.take(1)
    w4s, w4r = slots.take(NX), slots.take(NX)
    w5s, w5r = slots.take(NX), slots.take(NX)

    def space_y(t):
        return zh * 8 + rem(y + t, NY) * 2 + c

    def w1_start():
        for t in ORDER:
            send(mix.at[:, own_cols], wall.at[zl, x, :, own_cols], w1s + t, w1r + t, at(rem(zl + t, NZ), x, s))
        wall[zl, x, :, own_cols] = mix[:, own_cols]

    def w2_start():
        for t in ORDER:
            zf = rem(zl + NZ - t, NZ)
            recv(wall.at[zf, x, :, own_cols], w1r + t, at(zf, x, s))
        part = wall.at[:, x, :, own_cols]
        for t in range(1, NY):
            send(part, part, w2s + t, w2r + t, at(zl, x, space_y(t)))

    def w3_start():
        for t in range(1, NY):
            cols = lanes(128 * (c * 4 + rem(y + NY - t, NY)), 128)
            recv(wall.at[:, x, :, cols], w2r + t, at(zl, x, space_y(NY - t)))
        part = wall.at[:, x, :, side]
        send(part, part, w3s, w3r, at(zl, x, s_c))

    def w3_wait():
        recv(wall.at[:, x, :, other], w3r, at(zl, x, s_c))

    def w4_start():
        part = wall.at[:, x, :, side]
        for t in range(1, NX):
            send(part, part, w4s + t, w4r + t, at(zl, rem(x + t, NX), s))

    def w5_start():
        for t in range(1, NX):
            xf = rem(x + NX - t, NX)
            part = wall.at[:, xf, :, side]
            recv(part, w4r + t, at(zl, xf, s))
            send(part, part, w5s + t, w5r + t, at(zl, x, s_c))

    def w5_wait():
        for t in range(1, NX):
            xf = rem(x + NX - t, NX)
            recv(wall.at[:, xf, :, other], w5r + t, at(zl, x, s_c))

    lane = lax.broadcasted_iota(jnp.int32, (8, 8, 128), 2)
    first_col = lax.rem(lane, WW) == 0
    last_col = lax.rem(lane, WW) == WW - 1
    first_row = lane < WW
    zero = jnp.zeros((8, 8, 128), F32)

    def columns(v):
        before = jnp.where(first_col, zero, pltpu.roll(v, 1, 2))
        after = jnp.where(last_col, zero, pltpu.roll(v, 127, 2))
        return before, v, after

    def rows_down(v):
        swapped = pltpu.roll(v, WW, 2)
        above = jnp.concatenate([zero[:1], swapped[:-1]], axis=0)
        return jnp.where(first_row, above, swapped)

    def rows_up(v):
        swapped = pltpu.roll(v, WW, 2)
        below = jnp.concatenate([swapped[1:], zero[:1]], axis=0)
        return jnp.where(first_row, swapped, below)

    def conv(src, d, flip):
        @pl.loop(0, CH // 8)
        def _(g):
            rows = pl.ds(pl.multiple_of(8 * g, 8), 8)
            sums = [None] * 3
            for a in range(3):
                shifted = columns(src[pl.ds(8 * (d + a), 8), rows, :])
                for b in range(3):
                    for e in range(3):
                        tap = 9 * a + 3 * b + e
                        tap = 26 - tap if flip else tap
                        term = tb[tap, rows, :][None] * shifted[e]
                        sums[b] = term if sums[b] is None else sums[b] + term
            sp32[pl.ds(8 * d, 8), rows, :] = rows_down(sums[0]) + sums[1] + rows_up(sums[2])

    def widen(src, start, dst, chunk):
        for j in range(8):
            dst[chunk + j] = src[:, pl.ds(start + 128 * j, 128)].astype(F32)

    def pointwise(d):
        @pl.loop(0, 8)
        def _(j):
            at_chunk = 8 * d + j
            cells = lanes(128 * at_chunk, 128)
            spatial = sp32[at_chunk]
            sig = lax.logistic(spatial)
            grad = up[:, cells].astype(F32) * (sig * (1.0 + spatial * (1.0 - sig)))
            grad = grad.astype(BF16)
            sgb[:, cells] = grad
            sg32[8 + at_chunk] = grad.astype(F32)
            out[:, cells] = (vol[:, cells].astype(F32) + spatial * sig).astype(BF16)

    def forward_planes(first, step, count):
        @pl.loop(0, count)
        def _(i):
            d = first + step * i
            conv(m32, d, False)
            pointwise(d)

    def backward_planes(first, step):
        @pl.loop(0, 2)
        def _(i):
            d = first + step * i
            conv(sg32, d, True)

            @pl.loop(0, 8)
            def _(j):
                mgb[:, lanes(128 * (8 * d + j), 128)] = sp32[8 * d + j].astype(BF16)

    def tap_sums():
        @pl.loop(0, CH // 8)
        def _(g):
            rows = pl.ds(pl.multiple_of(8 * g, 8), 8)
            for tap in range(27):
                tg[tap, rows, :] = zero[0]

            @pl.loop(0, PLANES)
            def _(d):
                grad = sg32[pl.ds(8 * d + 8, 8), rows, :]
                grads = (rows_up(grad), grad, rows_down(grad))
                for a in range(3):
                    shifted = columns(m32[pl.ds(8 * (d + a), 8), rows, :])
                    for b in range(3):
                        for e in range(3):
                            tap = 9 * a + 3 * b + e
                            tg[tap, rows, :] = tg[tap, rows, :] + jnp.sum(grads[b] * shifted[e], axis=0)

        tap_lane = lax.broadcasted_iota(jnp.int32, (CH, 128), 1)
        total = jnp.zeros((CH, 128), F32)
        for tap in range(27):
            total = jnp.where(tap_lane == tap, jnp.sum(tg[tap], axis=1, keepdims=True), total)
        ts[0] = total

    halo_s = [slots.take(2), slots.take(2)]
    halo_r = [slots.take(2), slots.take(2)]
    has_low, has_high = s > 0, s < NS - 1
    sends_low, sends_high = (s > 0) & (s != 8), (s < NS - 1) & (s != 7)

    def halo_low(i, src, dst):
        return copy_to(src, dst, halo_s[i], halo_r[i], at(zl, x, s - 1))

    def halo_high(i, src, dst):
        return copy_to(src, dst, halo_s[i] + 1, halo_r[i] + 1, at(zl, x, s + 1))

    def m_low():
        return halo_low(0, mb.at[:, pl.ds(CELLS, CELLS)], mb.at[:, pl.ds(5 * CELLS, CELLS)])

    def m_high():
        return halo_high(0, mb.at[:, pl.ds(4 * CELLS, CELLS)], mb.at[:, pl.ds(0, CELLS)])

    def g_low():
        return halo_low(1, sgb.at[:, pl.ds(0, CELLS)], sgh.at[:, pl.ds(CELLS, CELLS)])

    def g_high():
        return halo_high(1, sgb.at[:, pl.ds(3 * CELLS, CELLS)], sgh.at[:, pl.ds(0, CELLS)])

    cross_s, cross_r = slots.take(NZ * CHUNKS), slots.take(2 * CHUNKS)
    cross_part = zl - 6 * (8 - s)
    cross_sends = ((s == 7) & (zl >= 6)) | ((s == 8) & (zl <= 1))

    def cross_copy(z, j):
        place = mb.at[:, lanes(5 * CELLS * (s - 7) + PART * cross_part + WIDTH * j, WIDTH)]
        return copy_to(mq.at[z, :, chunk(j)], place, cross_s + NZ * j + z,
                       cross_r + CHUNKS * cross_part + j, at(z, x, 15 - s))

    def cross_start(j):
        @pl.when(cross_sends)
        def _():
            for z in range(NZ):
                cross_copy(z, j).start()

    def cross_arrive(start, first_z):
        for part in range(2):
            for j in range(CHUNKS):
                recv(mb.at[:, pl.ds(start + PART * part + WIDTH * j, WIDTH)],
                     cross_r + CHUNKS * part + j, at(first_z + part, x, 15 - s))

    def mixed_halo_arrive():
        @pl.when((s > 0) & (s != 8))
        def _():
            recv(mb.at[:, pl.ds(0, CELLS)], halo_r[0] + 1, at(zl, x, s - 1))

        pl.when(s == 8)(lambda: cross_arrive(0, 6))

        @pl.when((s < NS - 1) & (s != 7))
        def _():
            recv(mb.at[:, pl.ds(5 * CELLS, CELLS)], halo_r[0], at(zl, x, s + 1))

        pl.when(s == 7)(lambda: cross_arrive(5 * CELLS, 0))
        for edge, start, row in ((s == 0, 0, 0), (s == NS - 1, 5 * CELLS, 40)):
            @pl.when(edge)
            def _():
                for j in range(8):
                    m32[row + j] = jnp.zeros((CH, 128), F32)

            @pl.when(jnp.logical_not(edge))
            def _():
                widen(mb, start, m32, row)

    def halo_arrive(i, low_ref, low_at, high_ref, high_at, dst):
        @pl.when(has_low)
        def _():
            recv(low_ref.at[:, pl.ds(low_at, CELLS)], halo_r[i] + 1, at(zl, x, s - 1))
            widen(low_ref, low_at, dst, 0)

        @pl.when(s == 0)
        def _():
            for j in range(8):
                dst[j] = jnp.zeros((CH, 128), F32)

        @pl.when(has_high)
        def _():
            recv(high_ref.at[:, pl.ds(high_at, CELLS)], halo_r[i], at(zl, x, s + 1))
            widen(high_ref, high_at, dst, 40)

        @pl.when(s == NS - 1)
        def _():
            for j in range(8):
                dst[40 + j] = jnp.zeros((CH, 128), F32)

    volume_gather = Gather(vol, vol_all)
    grad_gather = PlaneGather(mgb, mg_all)
    mixed_scatter = Scatter(mq, mb, CELLS)
    back_scatter = Scatter(bq, bb, 0)

    w1_start()
    volume_gather.start()
    for tap in range(27):
        tb[tap] = jnp.broadcast_to(taps[:, tap : tap + 1], (CH, 128))
    w2_start()
    other_half_to_column()
    for j in range(CHUNKS):
        volume_gather.arrive(j)
        if j == 1:
            w3_start()
    w3_wait()
    columns_own = wall[:, pl.ds(x, 1), :, :].reshape(NZ * CH, C)
    for j in range(CHUNKS):
        volume_gather.finish(j)
        multiply(columns_own, vol_all, j, mq)
        mixed_scatter.start(j)
        if j == 0:
            other_half_known()
        cross_start(j)
    w4_start()
    for z in (0, 1):
        mixed_scatter.wait(z)
    pl.when(sends_low)(lambda: m_low().start())
    for z in (6, 7):
        mixed_scatter.wait(z)
    pl.when(sends_high)(lambda: m_high().start())
    for z in (2, 3, 4, 5):
        mixed_scatter.wait(z)

    for d in range(PLANES):
        widen(mb, CELLS * (d + 1), m32, 8 * (d + 1))
    forward_planes(1, 1, 1)
    mixed_halo_arrive()
    forward_planes(0, 3, 2)
    pl.when(has_low)(lambda: g_low().start())
    pl.when(has_high)(lambda: g_high().start())
    w5_start()

    forward_planes(2, 1, 1)
    backward_planes(1, 1)
    grad_gather.start((3, 4, 2, 5))
    tap_sums()
    w5_wait()
    picked = lax.broadcasted_iota(jnp.int32, (CH, 128), 1) == (
        lax.broadcasted_iota(jnp.int32, (CH, 128), 0) + CH * x
    )
    picks = jnp.where(picked, 1.0, 0.0).astype(BF16)
    for z in range(NZ):
        block = wall[:, :, :, pl.ds(128 * z, 128)].reshape(C, 128)
        rows = lax.dot_general(picks, block, (((1,), (1,)), ((), ())), preferred_element_type=F32)
        wt[z] = rows.astype(BF16)

    halo_arrive(1, sgh, 0, sgh, CELLS, sg32)
    backward_planes(0, 3)
    grad_gather.start((0, 7, 1, 6))
    grad_gather.own()

    t1s, t1r = slots.take(1), slots.take(1)
    t2s, t2r = slots.take(NY), slots.take(NY)
    t3s, t3r = slots.take(1), slots.take(1)
    send(ts.at[0], tr.at[0], t1s, t1r, at(zl, x, s_c))

    def taps_y():
        recv(tr.at[0], t1r, at(zl, x, s_c))
        ts[1] = ts[0] + tr[0]
        for t in range(1, NY):
            send(ts.at[1], tr.at[1 + y], t2s + t, t2r + t, at(zl, x, space_y(t)))
        tr[1 + y] = ts[1]

    def taps_z():
        for t in range(1, NY):
            recv(tr.at[1 + rem(y + NY - t, NY)], t2r + t, at(zl, x, space_y(NY - t)))
        ts[2] = (tr[1] + tr[2]) + (tr[3] + tr[4])
        send(ts.at[2], tr.at[5], t3s, t3r, at(zl, x, s_h))

    for j in range(CHUNKS):
        grad_gather.arrive(j)
        if j == 0:
            taps_y()

    d1s, d1r = slots.take(1), slots.take(1)
    d2s, d2r = slots.take(2 * NY), slots.take(2 * NY)
    d3s, d3r = slots.take(NS), slots.take(NS)
    d4s_sem, d4r_sem = slots.take(1), slots.take(1)
    own_grad = mg_all[:, pl.ds(x, 1), :, :].reshape(NZ * CH, PART)
    for i in range(4):
        part = lax.dot_general(
            own_grad, vol_all[pl.ds(2 * i, 2)].reshape(C // 4, PART),
            (((1,), (1,)), ((), ())), preferred_element_type=F32,
        )
        part = part.reshape(NZ, 2, CH // 2, C // 4)
        dw[:, :, :, pl.ds(256 * i, 256)] = part
        dwb[:, :, :, pl.ds(256 * i, 256)] = part.astype(BF16)
    send(dwb.at[:, 1 - c], d1b, d1s, d1r, at(zl, x, s_c))
    taps_z()

    rows_own = wt[...].reshape(NZ * CH, C)

    def back(j):
        grad_gather.finish(j)
        multiply(rows_own, mg_all, j, bq)
        back_scatter.start(j)

    back(0)
    recv(d1b, d1r, at(zl, x, s_c))
    summed = d1b[...].astype(F32) + dw[:, pl.ds(c, 1)].reshape(NZ, CH // 2, C)
    d1[...] = summed
    a1b[...] = summed.astype(BF16)
    for t in range(1, NY):
        for h in range(2):
            cols = lanes(128 * (4 * h + rem(y + t, NY)), 128)
            send(a1b.at[:, :, cols], d2.at[t - 1, h], d2s + 2 * t + h, d2r + 2 * t + h, at(zl, x, space_y(t)))
    back(1)
    for h in range(2):
        summed = d1[:, :, lanes(128 * (4 * h + y), 128)]
        for t in range(1, NY):
            recv(d2.at[t - 1, h], d2r + 2 * t + h, at(zl, x, space_y(NY - t)))
            summed = summed + d2[t - 1, h].astype(F32)
        a2[h] = summed
        a2b[h] = summed.astype(BF16)
    z_own = zh * NZ + zl

    def ring(t):
        z = rem(z_own + t, NS)
        return div(z, NZ), rem(z, NZ)

    for t in (8, 7, 9, 6, 10, 5, 11, 4, 12, 3, 13, 2, 14, 1, 15):
        h, z = ring(t)
        send(a2b.at[h, z], d3.at[t - 1], d3s + t, d3r + t, at(z, x, h * 8 + y * 2 + c))
    back(2)
    back(3)
    total = a2[zh, zl]
    for t in range(1, NS):
        h, z = ring(NS - t)
        recv(d3.at[t - 1], d3r + t, at(z, x, h * 8 + y * 2 + c))
        total = total + d3[t - 1].astype(F32)
    d4s[...] = total
    send(d4s, d4r, d4s_sem, d4r_sem, at(zl, x, s_c))

    for z in range(NZ):
        back_scatter.wait(z)

    @pl.loop(0, SLAB // 128)
    def _(j):
        cells = lanes(128 * j, 128)
        vgrad[:, cells] = (up[:, cells].astype(F32) + bb[:, cells].astype(F32)).astype(BF16)

    recv(tr.at[5], t3r, at(zl, x, s_h))
    tgrad[...] = ((ts[2] + tr[5]) * norm)[:, :27]
    recv(d4r, d4r_sem, at(zl, x, s_c))
    even = c == 0
    full = jnp.concatenate(
        [jnp.where(even, d4s[...], d4r[...]), jnp.where(even, d4r[...], d4s[...])], axis=0
    )
    mgrad[...] = jnp.where(even, full[:, :64], full[:, 64:]) * norm

    for cp in pending:
        cp.wait_send()
    pl.when(sends_low)(lambda: m_low().wait_send())
    pl.when(sends_high)(lambda: m_high().wait_send())
    pl.when(has_low)(lambda: g_low().wait_send())
    pl.when(has_high)(lambda: g_high().wait_send())
    grad_gather.drain()

    @pl.when(cross_sends)
    def _():
        for j in range(CHUNKS):
            for z in range(NZ):
                cross_copy(z, j).wait_send()

    assert slots.used <= N_SEMS, slots.used


def body(volume, mixing, kernel_taps, upstream):
    norm = 1.0 / math.sqrt(PLANES * NS * CELLS)
    vmem = pl.BlockSpec(memory_space=pltpu.VMEM)
    scratch = [
        ((CH, SLAB), BF16),
        ((CH, SLAB), BF16),
        ((NZ, NX, CH, PART), BF16),
        ((NZ, NX, CH, PART), BF16),
        ((NZ, NX, CH, C), BF16),
        ((NZ, CH, C), BF16),
        ((NZ, CH, PART), BF16),
        ((NZ, CH, PART), BF16),
        ((CH, 6 * CELLS), BF16),
        ((48, CH, 128), F32),
        ((48, CH, 128), F32),
        ((32, CH, 128), F32),
        ((CH, SLAB), BF16),
        ((CH, 2 * CELLS), BF16),
        ((CH, SLAB), BF16),
        ((CH, SLAB), BF16),
        ((27, CH, 128), F32),
        ((27, CH, 128), F32),
        ((3, CH, 128), F32),
        ((6, CH, 128), F32),
        ((NZ, 2, CH // 2, C), F32),
        ((NZ, 2, CH // 2, C), BF16),
        ((NZ, CH // 2, C), F32),
        ((NZ, CH // 2, C), BF16),
        ((NZ, CH // 2, C), BF16),
        ((3, 2, NZ, CH // 2, 128), BF16),
        ((2, NZ, CH // 2, 128), F32),
        ((2, NZ, CH // 2, 128), BF16),
        ((NS - 1, CH // 2, 128), BF16),
        ((CH // 2, 128), F32),
        ((CH // 2, 128), F32),
    ]
    output, volume_grad, mixing_grad, taps_grad = pl.pallas_call(
        functools.partial(kernel, norm),
        out_shape=(
            jax.ShapeDtypeStruct((CH, SLAB), BF16),
            jax.ShapeDtypeStruct((CH, SLAB), BF16),
            jax.ShapeDtypeStruct((CH, C // NS), F32),
            jax.ShapeDtypeStruct((CH, 27), F32),
        ),
        in_specs=[vmem] * 4,
        out_specs=(vmem,) * 4,
        scratch_shapes=[pltpu.VMEM(*one) for one in scratch] + [pltpu.SemaphoreType.DMA((N_SEMS,)), pltpu.SemaphoreType.REGULAR((2,))],
        compiler_params=pltpu.CompilerParams(collective_id=0, has_side_effects=True),
        name="conv_block",
    )(volume, upstream, mixing, kernel_taps)

    def finish(o_ref, v_ref, m_ref, t_ref, out, vgrad, mgrad, tgrad):
        for i in range(0, CH, 8):
            rows = pl.ds(i, 8)
            out[rows] = (lambda v: v.reshape(8, PLANES, CELLS))(o_ref[rows])
            vgrad[rows] = (lambda v: v.reshape(8, PLANES, CELLS))(v_ref[rows])
        mgrad[...] = m_ref[...]
        tgrad[...] = t_ref[...]

    return pl.pallas_call(
        finish,
        out_shape=(
            jax.ShapeDtypeStruct((CH, PLANES, CELLS), BF16),
            jax.ShapeDtypeStruct((CH, PLANES, CELLS), BF16),
            jax.ShapeDtypeStruct((CH, C // NS), F32),
            jax.ShapeDtypeStruct((CH, 27), F32),
        ),
        in_specs=[vmem] * 4,
        out_specs=(vmem,) * 4,
        name="by_planes",
    )(output, volume_grad, mixing_grad, taps_grad)


def solution(mesh):
    channel_slab = P("filter", "space", None)
    return jax.shard_map(
        body,
        mesh=mesh,
        in_specs=(channel_slab, P("filter", None), P("filter", None), channel_slab),
        out_specs=(channel_slab, channel_slab, P("filter", "space"), P("filter", None)),
        check_vma=False,
    )
```
